32 devices in a mesh: pair: 8 (over z, x), row: 4 (over y, core).
Axes of the slice: x: 2, y: 2, z: 4, core: 2. Of those that a mesh axis runs over, the one named last changes fastest.
Arguments:
- features: bfloat16 [16, 4, 32, 1024], P('pair', 'row'), may hold values from -6 to 6
- src_ids: int32 [16], replicated, may hold values from 0 to 15
- tgt_ids: int32 [16], replicated, may hold values from 0 to 15
- image_slot: int32 [16], replicated, may hold values from 0 to 15, each once
- w_first: bfloat16 [81, 16, 1], replicated, may hold values from -0.625 to 0.625
- w_mid: bfloat16 [81, 16, 16], replicated, may hold values from -0.15625 to 0.15625
- w_last: bfloat16 [81, 1, 16], replicated, may hold values from -0.15625 to 0.15625
Outputs:
- matches: bfloat16 [16, 4, 32, 128], P('pair', 'row')
The draws below stay inside these ranges and needn't reach their ends.
All inputs are finite; a program needn't handle non-finite values.
Results may differ from the reference program's by a relative error of at most 0.012.
The reference program's roundings to bfloat16 on the way (of `normed`, `correlation`, `hidden_one` and `hidden_two`) count: a program that leaves them out, or rounds other values in their place, can miss the bound.
Values may be sent and summed in bfloat16 or wider, within the bound.
A program may use at most 64 MiB of HBM per device.

```python
import math
import jax
import jax.numpy as jnp
import numpy as np
from jax import lax

FEAT = 1024
CONV = 16
WID = 32
HGT = 4
IMAGES = 16
PAIRS = 16


def place_ends(drawn, own_key, smallest, top_value):
    spot = [jax.random.randint(jax.random.fold_in(own_key, axis), (), 0, length) for axis, length in enumerate(drawn.shape)]
    longest = drawn.shape.index(max(drawn.shape))
    beside = spot[:longest] + [(spot[longest] + 1) % drawn.shape[longest]] + spot[longest + 1:]
    return drawn.at[tuple(spot)].set(smallest).at[tuple(beside)].set(top_value)


def levels(key, extent, split, least, top_value):
    gain = 1.0
    for axis_at, parts in split:
        draws = jax.random.uniform(jax.random.fold_in(jax.random.fold_in(key, 6), axis_at), (parts,), jnp.float32, least / len(split), top_value / len(split))
        gain = gain * jnp.repeat(jnp.exp(draws), extent[axis_at] // parts).reshape((-1,) + (1,) * (len(extent) - 1 - axis_at))
    return gain


def rank_bounds(number_of, skew):
    portions = [(1 << 20) // math.isqrt(rank ** skew) + 1 for rank in range(1, number_of + 1)]
    spread = 1 + sum(portions) // (1 << 30)
    return np.cumsum(np.array([max(1, weight // spread) for weight in portions]))


def skewed_ids(own_key, extent, number_of, lean):
    grid = rank_bounds(number_of, lean)
    lot = jax.random.randint(jax.random.fold_in(own_key, 1), extent, 0, int(grid[number_of - 1]))
    grade = jnp.searchsorted(jnp.asarray(grid, jnp.int32), lot, side="right")
    return jax.random.permutation(jax.random.fold_in(own_key, 2), number_of)[grade].astype(jnp.int32)


def gaussian(rng, shape, spread, most, cuts=(), kind=jnp.bfloat16):
    entries = spread * jax.random.normal(rng, shape, jnp.float32)
    if cuts:
        entries = entries * levels(rng, shape, cuts, -0.22, 0.18)
    return jnp.clip(entries, -most, most).astype(kind)


def setup_inputs(seed: int = 0) -> dict:
    streams_of = jax.random.split(jax.random.key(seed), 8)
    return {
        "features": gaussian(streams_of[0], (IMAGES, HGT, WID, FEAT), 1.0, 6.0, ((0, 8), (1, 4))),
        "src_ids": place_ends(skewed_ids(streams_of[1], (PAIRS,), IMAGES, 2), jax.random.fold_in(streams_of[1], 3), 0, IMAGES - 1).astype(jnp.int32),
        "tgt_ids": place_ends(skewed_ids(streams_of[2], (PAIRS,), IMAGES, 1), jax.random.fold_in(streams_of[2], 3), 0, IMAGES - 1).astype(jnp.int32),
        "image_slot": jax.random.permutation(streams_of[3], IMAGES).astype(jnp.int32),
        "w_first": gaussian(streams_of[4], (81, CONV, 1), 81 ** -0.5, 0.625),
        "w_mid": gaussian(streams_of[5], (81, CONV, CONV), (81 * CONV) ** -0.5, 0.15625),
        "w_last": gaussian(streams_of[6], (81, 1, CONV), (81 * CONV) ** -0.5, 0.15625),
    }


EPSILON = 1e-05
NORM_EPS = 1e-06

def normalize(features):
    flattened = features.astype(jnp.float32)
    scale = lax.rsqrt(lax.optimization_barrier(jnp.sum(flattened * flattened, axis=-1, keepdims=True)) + NORM_EPS)
    return (flattened * scale).astype(jnp.bfloat16)

def consensus_layer(tensor, weight, is_last):
    channels_in = tensor.shape[0]
    channels_out = weight.shape[1]
    kernels = weight.astype(jnp.float32).reshape(3, 3, 3, 3, channels_out, channels_in)
    padded = jnp.pad(tensor.astype(jnp.float32), ((0, 0), (1, 1), (0, 0), (0, 0), (0, 0)))
    summed = jnp.zeros((HGT, channels_out, WID, HGT, WID), jnp.float32)
    for a in range(3):
        window = jnp.transpose(padded[:, a:a + HGT], (1, 0, 2, 3, 4))
        kernel = jnp.transpose(kernels[a], (3, 4, 0, 1, 2))
        summed = summed + lax.conv_general_dilated(window, kernel, (1, 1, 1), 'SAME', precision=lax.Precision.HIGHEST)
    result = jax.nn.relu(jnp.transpose(summed, (1, 0, 2, 3, 4)))
    if is_last:
        return result
    return result.astype(jnp.bfloat16)

def reference(features, src_ids, tgt_ids, image_slot, w_first, w_mid, w_last):
    normed = normalize(features)
    positions = HGT * WID

    def one_pair(pair_ids):
        source = normed[image_slot[pair_ids[0]]].reshape(positions, FEAT)
        target = normed[image_slot[pair_ids[1]]].reshape(positions, FEAT)
        correlation = jnp.dot(source, target.T, preferred_element_type=jnp.float32).astype(jnp.bfloat16)
        correlation = correlation.reshape(1, HGT, WID, HGT, WID)
        hidden_one = consensus_layer(correlation, w_first, False)
        hidden_two = consensus_layer(hidden_one, w_mid, False)
        consensus = consensus_layer(hidden_two, w_last, True)[0]
        source_best = lax.optimization_barrier(jnp.max(consensus, axis=(0, 1)))
        target_best = lax.optimization_barrier(jnp.max(consensus, axis=(2, 3), keepdims=True))
        matches = consensus / (source_best + EPSILON) * (consensus / (target_best + EPSILON))
        return matches.astype(jnp.bfloat16).reshape(HGT, WID, positions)
    return lax.map(one_pair, jnp.stack([src_ids, tgt_ids], axis=1))
```

```python
import jax
import jax.numpy as jnp
from jax import lax
from jax.experimental import pallas as pl
from jax.experimental.pallas import tpu as pltpu
from jax.sharding import PartitionSpec as P

WID = 32
HALVES = 2
VMEM_LIMIT = 16 << 20
MESH = pl.DeviceIdType.MESH


EPSILON = 1e-05
NORM_EPS = 1e-06


def with_halo(cells, sides, width):
    for axis, dim in sides:
        count = lax.axis_size(axis)
        ends = count - 1
        head = lax.slice_in_dim(cells, 0, width, axis=dim)
        tail = lax.slice_in_dim(cells, cells.shape[dim] - width, cells.shape[dim], axis=dim)
        cells = jnp.concatenate(
            [
                lax.ppermute(tail, axis, [(i, (i + 1) % count) for i in range(ends)]),
                cells,
                lax.ppermute(head, axis, [((i + 1) % count, i) for i in range(ends)]),
            ],
            axis=dim,
        )
    return cells


def slot_lookup(image_ids, image_slot):
    matches = image_ids[..., None] == jnp.arange(image_slot.shape[0], dtype=jnp.int32)
    return jnp.sum(jnp.where(matches, image_slot, 0), axis=-1)


def consensus_layer(tensor, weight, col_masks, is_last):
    group_pairs = tensor.shape[0]
    channels_in = tensor.shape[1]
    positions = tensor.shape[4]
    channels_out = weight.shape[1]
    rimmed = with_halo(tensor, (("row", 2),), 1)
    padded = jnp.pad(rimmed, ((0, 0), (0, 0), (0, 0), (1, 1), (0, 0)))
    matrix = (
        weight.reshape(9, 9, channels_out, channels_in)
        .transpose(1, 2, 0, 3)
        .reshape(9 * channels_out, 9 * channels_in)
    )
    results = []
    for member in range(group_pairs):
        stacked = jnp.stack(
            [padded[member, :, a, b : b + WID, :] for a in range(3) for b in range(3)]
        )
        product = jnp.dot(
            matrix,
            stacked.reshape(9 * channels_in, WID * positions),
            preferred_element_type=jnp.float32,
        )
        product = product.reshape(9, channels_out, WID, positions)
        summed = jnp.zeros((channels_out, WID, positions), jnp.float32)
        for c in range(3):
            for d in range(3):
                offset = (c - 1) * WID + (d - 1)
                widened = jnp.pad(product[c * 3 + d], ((0, 0), (0, 0), (WID + 1, WID + 1)))
                shifted = widened[:, :, WID + 1 + offset : WID + 1 + offset + positions]
                summed = summed + shifted * col_masks[d]
        outputs = [jax.nn.relu(summed)]
        results.append(jnp.stack(outputs, axis=1))
    result = jnp.stack(results, axis=0)
    if is_last:
        return result
    return result.astype(jnp.bfloat16)


def local(features, src_ids, tgt_ids, image_slot, w_first, w_mid, w_last):
    local_images, local_rows, columns, channels = features.shape
    block_rows = local_rows * columns
    flattened = features.reshape(local_images, block_rows, channels).astype(jnp.float32)
    scale = lax.rsqrt(jnp.sum(flattened * flattened, axis=-1, keepdims=True) + NORM_EPS)
    normed = (flattened * scale).astype(jnp.bfloat16)
    group_pairs = src_ids.shape[0] // lax.axis_size("pair")
    pair_index = lax.axis_index("pair")
    wanted_ids = jnp.stack([src_ids, tgt_ids], axis=1)
    own_ids = lax.dynamic_slice_in_dim(
        wanted_ids, pair_index * group_pairs, group_pairs, 0
    ).reshape(-1)
    needed = slot_lookup(own_ids, image_slot)
    shard_piece = lax.all_gather(normed, "pair", axis=0, tiled=True)
    length = shard_piece.shape[0]
    one_hot = (needed[:, None] == jnp.arange(length, dtype=jnp.int32)).astype(jnp.bfloat16)
    chosen = jnp.einsum("wk,krc->wrc", one_hot, shard_piece, preferred_element_type=jnp.float32)
    routed = chosen.astype(jnp.bfloat16)
    routed = routed.reshape(group_pairs, 2, block_rows, channels)
    sources = routed[:, 0]
    targets = routed[:, 1]
    correlation = jnp.einsum(
        "prc,ptc->prt",
        sources,
        lax.all_gather(targets, "row", axis=1, tiled=True),
        preferred_element_type=jnp.float32,
    )
    positions = correlation.shape[2]
    tensor = correlation.astype(jnp.bfloat16).reshape(
        group_pairs, 1, local_rows, columns, positions
    )
    target_col = jnp.arange(positions, dtype=jnp.int32) % WID
    col_masks = [
        ((target_col + d - 1 >= 0) & (target_col + d - 1 < WID)).astype(jnp.float32)
        for d in range(3)
    ]
    hidden_one = consensus_layer(tensor, w_first, col_masks, False)
    hidden_two = consensus_layer(hidden_one, w_mid, col_masks, False)
    consensus = consensus_layer(hidden_two, w_last, col_masks, True)[:, 0]
    target_best = jnp.max(consensus, axis=-1, keepdims=True)
    local_best = jnp.max(consensus, axis=(1, 2))
    source_best = lax.pmax(local_best, "row")
    matches = (
        consensus
        / (source_best[:, None, None, :] + EPSILON)
        * (consensus / (target_best + EPSILON))
    )
    return matches.astype(jnp.bfloat16)


def spread_kernel(
    x_any, wf_any, wm_any, wl_any, src_any, tgt_any, slot_any, o_ref,
    x_ref, wf_ref, wm_ref, wl_ref, src_ref, tgt_ref, slot_ref, load_sem,
    w1_ref, w2_ref, w3_ref, moves,
    parts, held, picked, chosen, partial, other, grid, taps, first, second, third,
    scores, best, got_scores, got_best,
    hop_send, hop_recv, pick_send, pick_recv, mate_sem, score_send, score_recv, best_send, best_recv,
):
    groups = lax.axis_size("pair")
    rows = lax.axis_size("row")
    me = lax.axis_index("pair")
    row = lax.axis_index("row")
    group_pairs = rows // HALVES
    team = lax.div(row, HALVES)
    half = lax.rem(row, HALVES)
    local_images, columns, chunk = parts.shape[1:]
    positions = rows * columns
    lanes = o_ref.shape[3]
    depth = wm_ref.shape[0]
    band = rows * depth
    slots = grid.shape[1]
    share = columns // HALVES
    kept = grid.shape[0]
    reach_one, reach_two = share + 4, share + 2

    barrier = pltpu.get_barrier_semaphore()
    for step in range(1, groups):
        pl.semaphore_signal(
            barrier, inc=1, device_id={"pair": lax.rem(me + step, groups)}, device_id_type=MESH
        )
    for turn in range(1, rows):
        pl.semaphore_signal(
            barrier, inc=1, device_id={"row": lax.rem(row + turn, rows)}, device_id_type=MESH
        )
    loads = [
        pltpu.make_async_copy(source, target, load_sem.at[n])
        for n, (source, target) in enumerate(
            (
                (x_any, x_ref), (wf_any, wf_ref), (wm_any, wm_ref), (wl_any, wl_ref),
                (src_any, src_ref), (tgt_any, tgt_ref), (slot_any, slot_ref),
            )
        )
    ]
    for load in loads:
        load.start()
    loads[0].wait()

    for image in range(local_images):
        cells = x_ref[image, 0].astype(jnp.float32)
        scale = lax.rsqrt(jnp.sum(cells * cells, axis=-1, keepdims=True) + NORM_EPS)
        normed = (cells * scale).astype(jnp.bfloat16)
        for piece in range(groups):
            parts[piece, image] = normed[:, piece * chunk : (piece + 1) * chunk]
    held[pl.ds(me * local_images, local_images)] = parts[me]
    pl.semaphore_wait(barrier, groups + rows - 2)

    def hop(peer, slot):
        return pltpu.make_async_remote_copy(
            src_ref=parts.at[peer],
            dst_ref=held.at[pl.ds(slot * local_images, local_images)],
            send_sem=hop_send.at[peer], recv_sem=hop_recv.at[slot],
            device_id={"pair": peer}, device_id_type=MESH,
        )

    order = list(range(1, groups))
    for step in order:
        hop(lax.rem(me + step, groups), me).start()

    grid[...] = jnp.zeros_like(grid)
    block = taps.shape[0] // (kept + 2)
    for edge in (0, kept + 1):
        taps[edge * block : (edge + 1) * block, :] = jnp.zeros((block, lanes), taps.dtype)
    for edge in (0, reach_one + 1):
        first[edge * band : (edge + 1) * band, :] = jnp.zeros((band, lanes), first.dtype)
    for edge in (0, reach_two + 1):
        second[edge * band : (edge + 1) * band, :] = jnp.zeros((band, lanes), second.dtype)

    def select(shape, test):
        i = lax.broadcasted_iota(jnp.int32, shape, 0)
        m = lax.broadcasted_iota(jnp.int32, shape, 1)
        return test(i, m)

    for tap in range(block // slots):
        c, d = tap // 3, tap % 3

        def reaches(i, m):
            line = lax.div(m, columns) + c - 1
            spot = lax.rem(m, columns) + d - 1
            return (i == line * columns + spot) & (line >= 0) & (line < rows) & (spot >= 0) & (spot < columns)

        if tap < 9:
            move = select((lanes, lanes), reaches).astype(jnp.bfloat16)
        else:
            move = jnp.zeros((lanes, lanes), jnp.bfloat16)
        moves[:, tap * lanes : (tap + 1) * lanes] = move

    for load in loads[1:]:
        load.wait()
    count = wf_ref.shape[1]
    kernels = jnp.concatenate([wm_ref[...].reshape(depth * depth, count), wl_ref[...]], axis=0)
    height = kernels.shape[0]
    wide = 2 * lanes
    matching = select((height, wide), lambda i, m: lax.rem(i, depth) == lax.rem(m, depth))
    folding = select((32, height), lambda i, m: lax.div(m, depth) == i).astype(jnp.bfloat16)
    line_of = select((32, wide), lambda i, m: lax.div(lax.rem(m, band), depth))
    last_rows = [[] for _ in range(rows)]
    for tap in range(9):
        here = select(
            (count, wide),
            lambda i, m: (i == (lax.div(lax.rem(m, band), depth) * 3 + lax.div(m, band)) * 9 + tap)
            & (lax.rem(m, band) < 3 * depth)
            & (m < 3 * band),
        ).astype(jnp.bfloat16)
        picks = jnp.dot(kernels, here, preferred_element_type=jnp.float32)
        picks = jnp.where(matching, picks, 0.0).astype(jnp.bfloat16)
        folded = jnp.dot(folding, picks, preferred_element_type=jnp.float32)
        for turn in range(rows):
            shift = ((turn - 1) * depth) % wide
            moved = pltpu.roll(folded, shift, 1) if shift else folded
            moved = jnp.where((line_of >= turn - 1) & (line_of <= turn + 1), moved, 0.0)[:, : 3 * band]
            start = (turn * 9 + tap) * depth
            w2_ref[start : start + depth, :] = moved[:depth].astype(jnp.bfloat16)
            last_rows[turn].append(moved[depth : depth + 1])
    for turn in range(rows):
        last = jnp.concatenate(last_rows[turn] + [jnp.zeros((16 - 9, 3 * band), jnp.float32)], axis=0)
        w3_ref[turn * 16 : (turn + 1) * 16, :] = last.astype(jnp.bfloat16)

    for turn in range(rows):
        def uses(i, m):
            inside = lax.rem(m, block)
            a = lax.rem(inside, slots) - turn + 1
            tap = lax.div(inside, slots)
            return (i == 27 * a + 9 * lax.div(m, block) + tap) & (a >= 0) & (a < 3) & (tap < 9)

        here = select((count, 3 * block), uses).astype(jnp.bfloat16)
        packed = jnp.dot(wf_ref[...], here, preferred_element_type=jnp.float32)
        w1_ref[turn * depth : (turn + 1) * depth, :] = packed.astype(jnp.bfloat16)

    def masks(size):
        place = lax.broadcasted_iota(jnp.int32, (size, lanes), 1)
        line = lax.div(place, columns)
        spot = lax.rem(place, columns)
        lines = [((line + c - 1 >= 0) & (line + c - 1 < rows)).astype(jnp.float32) for c in range(3)]
        spots = [((spot + d - 1 >= 0) & (spot + d - 1 < columns)).astype(jnp.float32) for d in range(3)]
        return lines, spots

    def gathered(term_at, lines, spots):
        summed = None
        for c in range(3):
            inner = None
            for d in range(3):
                term = term_at(c * 3 + d)
                if d != 1:
                    term = pltpu.roll(term, (1 - d) % lanes, 1) * spots[d]
                inner = term if inner is None else inner + term
            if c != 1:
                inner = pltpu.roll(inner, ((1 - c) * columns) % lanes, 1) * lines[c]
            summed = inner if summed is None else summed + inner
        return jnp.maximum(summed, 0.0)

    for step in order:
        source = lax.rem(me + groups - step, groups)
        hop(source, source).wait_recv()

    lot = lax.div(me, HALVES)
    side = lax.rem(me, HALVES)

    def pick(to, pair):
        return pltpu.make_async_remote_copy(
            src_ref=picked.at[to, pair], dst_ref=chosen.at[lot, row],
            send_sem=pick_send.at[to, pair], recv_sem=pick_recv.at[lot, row],
            device_id={"pair": to, "row": pair * HALVES + side}, device_id_type=MESH,
        )

    for step in order + [0]:
        to = lax.rem(me + step, groups)
        for pair in range(group_pairs):
            index = to * group_pairs + pair
            source_image = held[slot_ref[src_ref[index]]]
            target_image = held[slot_ref[tgt_ref[index]]]
            picked[to, pair, 0] = source_image
            picked[to, pair, 1] = target_image
            if step:
                pick(to, pair).start()
            else:
                @pl.when(pair * HALVES + side != row)
                def _():
                    pick(to, pair).start()

                @pl.when(pair * HALVES + side == row)
                def _():
                    chosen[lot, row, 0] = source_image
                    chosen[lot, row, 1] = target_image

    total = jnp.zeros((positions, positions), jnp.float32)
    for piece in range(groups // HALVES):
        source = piece * HALVES + half
        for turn in range(rows):
            @pl.when((source != me) | (row != turn))
            def _():
                pltpu.make_async_remote_copy(
                    src_ref=picked.at[0, 0], dst_ref=chosen.at[piece, turn],
                    send_sem=pick_send.at[0, 0], recv_sem=pick_recv.at[piece, turn],
                    device_id={"pair": source, "row": turn}, device_id_type=MESH,
                ).wait_recv()

        left = jnp.concatenate([chosen[piece, turn, 0] for turn in range(rows)], axis=0)
        right = jnp.concatenate([chosen[piece, turn, 1] for turn in range(rows)], axis=0)
        total = total + lax.dot_general(
            left, right, (((1,), (1,)), ((), ())), preferred_element_type=jnp.float32
        )
    partial[...] = total.reshape(partial.shape)
    off = columns - kept
    swap = pltpu.make_async_remote_copy(
        src_ref=partial.at[:, pl.ds(pl.multiple_of((1 - half) * off, off), kept)],
        dst_ref=other, send_sem=mate_sem.at[0], recv_sem=mate_sem.at[1],
        device_id={"row": row + 1 - 2 * half}, device_id_type=MESH,
    )
    swap.start()
    swap.wait()
    mine = partial[:, pl.ds(pl.multiple_of(half * off, off), kept), :]
    correlation = (mine + other[...]).astype(jnp.bfloat16).astype(jnp.float32)
    for turn in range(rows):
        grid[:, turn, :] = correlation[turn]
    cells = grid[...].reshape(kept * slots, lanes).astype(jnp.bfloat16)
    for pack in range(block // 16):
        shifted = jnp.dot(
            cells, moves[:, pack * 2 * lanes : (pack + 1) * 2 * lanes], preferred_element_type=jnp.float32
        )
        for j in range(kept):
            piece = shifted[j * slots : (j + 1) * slots]
            both = jnp.concatenate([piece[:, :lanes], piece[:, lanes:]], axis=0)
            start = (j + 1) * block + pack * 16
            taps[start : start + 16, :] = both.astype(jnp.bfloat16)

    def windows(ref, size, first_at):
        return jnp.concatenate(
            [ref[pl.ds(pl.multiple_of((first_at + n) * size, 16), 3 * size), :] for n in range(2)], axis=1
        )

    lead_one = half * (columns - reach_one - off)
    for t in range(0, reach_one, 2):
        product = jnp.dot(w1_ref[...], windows(taps, block, lead_one + t), preferred_element_type=jnp.float32)
        value = jnp.maximum(product, 0.0).astype(jnp.bfloat16)
        for n in range(2):
            first[(t + n + 1) * band : (t + n + 2) * band, :] = value[:, n * lanes : (n + 1) * lanes]

    lines, spots = masks(depth)
    for t in range(0, reach_two, 2):
        window = windows(first, band, 2 * half + t)
        for turn in range(rows):
            product = jnp.dot(
                w2_ref[turn * 9 * depth : (turn + 1) * 9 * depth, :], window, preferred_element_type=jnp.float32
            )
            for n in range(2):
                value = gathered(
                    lambda tap: product[tap * depth : (tap + 1) * depth, n * lanes : (n + 1) * lanes], lines, spots
                )
                start = (t + n + 1) * band + turn * depth
                second[start : start + depth, :] = value.astype(jnp.bfloat16)

    for t in range(0, share, 2):
        product = jnp.dot(w3_ref[...], windows(second, band, 2 * half + t), preferred_element_type=jnp.float32)
        for n in range(2):
            third[t + n] = product[:, n * lanes : (n + 1) * lanes]

    lines, spots = masks(share)
    peak = None
    for turn in range(rows):
        value = gathered(lambda tap: third[:, turn * 16 + tap, :], lines, spots)
        scores[turn] = value
        top = jnp.max(value, axis=0, keepdims=True)
        peak = top if peak is None else jnp.maximum(peak, top)
    peak = jnp.broadcast_to(peak, best.shape)
    best[...] = peak
    got_best[team, half] = peak

    def tell(turn):
        to = lax.rem(row + turn, rows)
        return pltpu.make_async_remote_copy(
            src_ref=best, dst_ref=got_best.at[team, half],
            send_sem=best_send.at[turn], recv_sem=best_recv.at[team, half],
            device_id={"row": to}, device_id_type=MESH,
        )

    def give(turn):
        to = lax.rem(row + turn, rows)
        return pltpu.make_async_remote_copy(
            src_ref=scores.at[to], dst_ref=got_scores.at[team, half],
            send_sem=score_send.at[turn], recv_sem=score_recv.at[team, half],
            device_id={"row": to}, device_id_type=MESH,
        )

    for turn in range(1, rows):
        give(turn).start()
        tell(turn).start()
    got_scores[team, half] = scores[row]

    for pair in range(group_pairs):
        for part in range(HALVES):
            origin = pair * HALVES + part

            @pl.when(origin != row)
            def _():
                pltpu.make_async_remote_copy(
                    src_ref=best, dst_ref=got_best.at[pair, part],
                    send_sem=best_send.at[1], recv_sem=best_recv.at[pair, part],
                    device_id={"row": origin}, device_id_type=MESH,
                ).wait_recv()
                pltpu.make_async_remote_copy(
                    src_ref=scores.at[0], dst_ref=got_scores.at[pair, part],
                    send_sem=score_send.at[1], recv_sem=score_recv.at[pair, part],
                    device_id={"row": origin}, device_id_type=MESH,
                ).wait_recv()

        source_best = got_best[pair, 0, 0:1, :]
        for part in range(1, HALVES):
            source_best = jnp.maximum(source_best, got_best[pair, part, 0:1, :])
        for part in range(HALVES):
            value = got_scores[pair, part]
            target_best = jnp.max(value, axis=-1, keepdims=True)
            o_ref[pair, 0, part * share : (part + 1) * share, :] = (
                value / (source_best + EPSILON) * (value / (target_best + EPSILON))
            ).astype(o_ref.dtype)

    for step in order:
        hop(lax.rem(me + step, groups), me).wait_send()
    for step in order + [0]:
        to = lax.rem(me + step, groups)
        for pair in range(group_pairs):
            if step:
                pick(to, pair).wait_send()
            else:
                @pl.when(pair * HALVES + side != row)
                def _():
                    pick(to, pair).wait_send()
    for turn in range(1, rows):
        give(turn).wait_send()
        tell(turn).wait_send()


def spread(features, src_ids, tgt_ids, image_slot, w_first, w_mid, w_last):
    groups = lax.axis_size("pair")
    rows = lax.axis_size("row")
    local_images, _, columns, channels = features.shape
    chunk = channels // groups
    depth = w_mid.shape[1]
    group_pairs = src_ids.shape[0] // groups
    positions = rows * columns
    band = rows * depth
    share = columns // HALVES
    kept = share + 8
    slots = 8
    block = 10 * slots
    vmem = pl.BlockSpec(memory_space=pltpu.VMEM)
    dma = pltpu.SemaphoreType.DMA
    bf16, f32 = jnp.bfloat16, jnp.float32
    weights = (w_first.transpose(2, 1, 0)[0], w_mid.transpose(1, 2, 0), w_last.transpose(1, 2, 0)[0])
    result = pl.pallas_call(
        spread_kernel,
        out_shape=pltpu.VMEM((group_pairs, 1, columns, positions), f32),
        in_specs=[pl.BlockSpec(memory_space=pltpu.HBM)] * 7,
        out_specs=vmem,
        scratch_shapes=[
            pltpu.VMEM(features.shape, bf16),
            *(pltpu.VMEM(weight.shape, bf16) for weight in weights),
            *(pltpu.SMEM(ids.shape, jnp.int32) for ids in (src_ids, tgt_ids, image_slot)),
            dma((7,)),
            pltpu.VMEM((band, 3 * block), bf16),
            pltpu.VMEM((9 * band, 3 * band), bf16),
            pltpu.VMEM((rows * 16, 3 * band), bf16),
            pltpu.VMEM((positions, 10 * positions), bf16),
            pltpu.VMEM((groups, local_images, columns, chunk), bf16),
            pltpu.VMEM((groups * local_images, columns, chunk), bf16),
            pltpu.VMEM((groups, group_pairs, 2, columns, chunk), bf16),
            pltpu.VMEM((groups // HALVES, rows, 2, columns, chunk), bf16),
            pltpu.VMEM((rows, columns, positions), f32),
            pltpu.VMEM((rows, kept, positions), f32),
            pltpu.VMEM((kept, slots, positions), f32),
            pltpu.VMEM(((kept + 2) * block, positions), bf16),
            pltpu.VMEM(((share + 6) * band, positions), bf16),
            pltpu.VMEM(((share + 4) * band, positions), bf16),
            pltpu.VMEM((share, rows * 16, positions), f32),
            pltpu.VMEM((rows, share, positions), f32),
            pltpu.VMEM((8, positions), f32),
            pltpu.VMEM((group_pairs, HALVES, share, positions), f32),
            pltpu.VMEM((group_pairs, HALVES, 8, positions), f32),
            dma((groups,)), dma((groups,)),
            dma((groups, group_pairs)), dma((groups // HALVES, rows)),
            dma((2,)),
            dma((rows,)), dma((group_pairs, HALVES)),
            dma((rows,)), dma((group_pairs, HALVES)),
        ],
        compiler_params=pltpu.CompilerParams(
            collective_id=0, has_side_effects=True, vmem_limit_bytes=VMEM_LIMIT
        ),
    )(*(pltpu.with_memory_space_constraint(x, pltpu.HBM) for x in (features, *weights, src_ids, tgt_ids, image_slot)))
    return result.astype(bf16)


def program(features, src_ids, tgt_ids, image_slot, w_first, w_mid, w_last):
    groups = lax.axis_size("pair")
    rows = lax.axis_size("row")
    _, local_rows, columns, channels = features.shape
    fits = (
        local_rows == 1
        and groups % HALVES == 0
        and rows * groups == HALVES * src_ids.shape[0]
        and channels % (groups * 128) == 0
        and rows * columns == 128
        and columns == 32
        and rows == 2 * HALVES
        and w_mid.shape[1] == 16
    )
    run = spread if fits else local
    return run(features, src_ids, tgt_ids, image_slot, w_first, w_mid, w_last)


def solution(mesh):
    placed = (P("pair", "row", None, None), P(), P(), P(), P(), P(), P())
    return jax.shard_map(
        program, mesh=mesh, in_specs=placed, out_specs=P("pair", "row", None, None), check_vma=False
    )
```

```python
import jax
import jax.numpy as jnp
from jax import lax
from jax.experimental import pallas as pl
from jax.experimental.pallas import tpu as pltpu
from jax.sharding import PartitionSpec as P

WID = 32
HALVES = 2
VMEM_LIMIT = 16 << 20
MESH = pl.DeviceIdType.MESH


EPSILON = 1e-05
NORM_EPS = 1e-06


def with_halo(cells, sides, width):
    for axis, dim in sides:
        count = lax.axis_size(axis)
        ends = count - 1
        head = lax.slice_in_dim(cells, 0, width, axis=dim)
        tail = lax.slice_in_dim(cells, cells.shape[dim] - width, cells.shape[dim], axis=dim)
        cells = jnp.concatenate(
            [
                lax.ppermute(tail, axis, [(i, (i + 1) % count) for i in range(ends)]),
                cells,
                lax.ppermute(head, axis, [((i + 1) % count, i) for i in range(ends)]),
            ],
            axis=dim,
        )
    return cells


def slot_lookup(image_ids, image_slot):
    matches = image_ids[..., None] == jnp.arange(image_slot.shape[0], dtype=jnp.int32)
    return jnp.sum(jnp.where(matches, image_slot, 0), axis=-1)


def consensus_layer(tensor, weight, col_masks, is_last):
    group_pairs = tensor.shape[0]
    channels_in = tensor.shape[1]
    positions = tensor.shape[4]
    channels_out = weight.shape[1]
    rimmed = with_halo(tensor, (("row", 2),), 1)
    padded = jnp.pad(rimmed, ((0, 0), (0, 0), (0, 0), (1, 1), (0, 0)))
    matrix = (
        weight.reshape(9, 9, channels_out, channels_in)
        .transpose(1, 2, 0, 3)
        .reshape(9 * channels_out, 9 * channels_in)
    )
    results = []
    for member in range(group_pairs):
        stacked = jnp.stack(
            [padded[member, :, a, b : b + WID, :] for a in range(3) for b in range(3)]
        )
        product = jnp.dot(
            matrix,
            stacked.reshape(9 * channels_in, WID * positions),
            preferred_element_type=jnp.float32,
        )
        product = product.reshape(9, channels_out, WID, positions)
        summed = jnp.zeros((channels_out, WID, positions), jnp.float32)
        for c in range(3):
            for d in range(3):
                offset = (c - 1) * WID + (d - 1)
                widened = jnp.pad(product[c * 3 + d], ((0, 0), (0, 0), (WID + 1, WID + 1)))
                shifted = widened[:, :, WID + 1 + offset : WID + 1 + offset + positions]
                summed = summed + shifted * col_masks[d]
        outputs = [jax.nn.relu(summed)]
        results.append(jnp.stack(outputs, axis=1))
    result = jnp.stack(results, axis=0)
    if is_last:
        return result
    return result.astype(jnp.bfloat16)


def local(features, src_ids, tgt_ids, image_slot, w_first, w_mid, w_last):
    local_images, local_rows, columns, channels = features.shape
    block_rows = local_rows * columns
    flattened = features.reshape(local_images, block_rows, channels).astype(jnp.float32)
    scale = lax.rsqrt(jnp.sum(flattened * flattened, axis=-1, keepdims=True) + NORM_EPS)
    normed = (flattened * scale).astype(jnp.bfloat16)
    group_pairs = src_ids.shape[0] // lax.axis_size("pair")
    pair_index = lax.axis_index("pair")
    wanted_ids = jnp.stack([src_ids, tgt_ids], axis=1)
    own_ids = lax.dynamic_slice_in_dim(
        wanted_ids, pair_index * group_pairs, group_pairs, 0
    ).reshape(-1)
    needed = slot_lookup(own_ids, image_slot)
    shard_piece = lax.all_gather(normed, "pair", axis=0, tiled=True)
    length = shard_piece.shape[0]
    one_hot = (needed[:, None] == jnp.arange(length, dtype=jnp.int32)).astype(jnp.bfloat16)
    chosen = jnp.einsum("wk,krc->wrc", one_hot, shard_piece, preferred_element_type=jnp.float32)
    routed = chosen.astype(jnp.bfloat16)
    routed = routed.reshape(group_pairs, 2, block_rows, channels)
    sources = routed[:, 0]
    targets = routed[:, 1]
    correlation = jnp.einsum(
        "prc,ptc->prt",
        sources,
        lax.all_gather(targets, "row", axis=1, tiled=True),
        preferred_element_type=jnp.float32,
    )
    positions = correlation.shape[2]
    tensor = correlation.astype(jnp.bfloat16).reshape(
        group_pairs, 1, local_rows, columns, positions
    )
    target_col = jnp.arange(positions, dtype=jnp.int32) % WID
    col_masks = [
        ((target_col + d - 1 >= 0) & (target_col + d - 1 < WID)).astype(jnp.float32)
        for d in range(3)
    ]
    hidden_one = consensus_layer(tensor, w_first, col_masks, False)
    hidden_two = consensus_layer(hidden_one, w_mid, col_masks, False)
    consensus = consensus_layer(hidden_two, w_last, col_masks, True)[:, 0]
    target_best = jnp.max(consensus, axis=-1, keepdims=True)
    local_best = jnp.max(consensus, axis=(1, 2))
    source_best = lax.pmax(local_best, "row")
    matches = (
        consensus
        / (source_best[:, None, None, :] + EPSILON)
        * (consensus / (target_best + EPSILON))
    )
    return matches.astype(jnp.bfloat16)


def spread_kernel(
    x_any, wf_any, wm_any, wl_any, src_any, tgt_any, slot_any, o_ref,
    x_ref, wf_ref, wm_ref, wl_ref, src_ref, tgt_ref, slot_ref, load_sem,
    w1_ref, w2_ref, w3_ref, moves,
    parts, held, picked, chosen, partial, other, grid, taps, first, second, third,
    scores, best, got_scores, got_best,
    hop_send, hop_recv, pick_send, pick_recv, mate_sem, score_send, score_recv, best_send, best_recv,
):
    groups = lax.axis_size("pair")
    rows = lax.axis_size("row")
    me = lax.axis_index("pair")
    row = lax.axis_index("row")
    group_pairs = rows // HALVES
    team = lax.div(row, HALVES)
    half = lax.rem(row, HALVES)
    local_images, columns, chunk = parts.shape[1:]
    positions = rows * columns
    lanes = o_ref.shape[3]
    depth = wm_ref.shape[0]
    band = rows * depth
    slots = grid.shape[1]
    share = columns // HALVES
    kept = grid.shape[0]
    reach_one, reach_two = share + 4, share + 2

    low, high = me, groups - 1 - me
    near, gap = jnp.minimum(low, high), jnp.abs(high - low)

    def distant(step):
        single = jnp.where(high > low, groups - 1 - step, step)
        beyond = step - gap
        away = near - lax.div(beyond, 2)
        double = me + jnp.where(lax.rem(beyond, 2) == 0, away, -away)
        return jnp.where(step < gap, single, double)

    peers = [distant(step) for step in range(groups - 1)]
    routes = [jnp.where(k < me, k, k + 1) for k in range(groups - 1)]

    barrier = pltpu.get_barrier_semaphore()
    for to in peers:
        pl.semaphore_signal(barrier, inc=1, device_id={"pair": to}, device_id_type=MESH)
    for turn in range(1, rows):
        pl.semaphore_signal(
            barrier, inc=1, device_id={"row": lax.rem(row + turn, rows)}, device_id_type=MESH
        )
    loads = [
        pltpu.make_async_copy(source, target, load_sem.at[n])
        for n, (source, target) in enumerate(
            (
                (x_any, x_ref), (wf_any, wf_ref), (wm_any, wm_ref), (wl_any, wl_ref),
                (src_any, src_ref), (tgt_any, tgt_ref), (slot_any, slot_ref),
            )
        )
    ]
    for load in loads:
        load.start()
    loads[0].wait()

    for image in range(local_images):
        cells = x_ref[image, 0].astype(jnp.float32)
        scale = lax.rsqrt(jnp.sum(cells * cells, axis=-1, keepdims=True) + NORM_EPS)
        normed = (cells * scale).astype(jnp.bfloat16)
        for piece in range(groups):
            parts[piece, image] = normed[:, piece * chunk : (piece + 1) * chunk]
    held[pl.ds(me * local_images, local_images)] = parts[me]
    pl.semaphore_wait(barrier, groups + rows - 2)

    def hop(peer, slot):
        return pltpu.make_async_remote_copy(
            src_ref=parts.at[peer],
            dst_ref=held.at[pl.ds(slot * local_images, local_images)],
            send_sem=hop_send.at[peer], recv_sem=hop_recv.at[slot],
            device_id={"pair": peer}, device_id_type=MESH,
        )

    for to in peers:
        hop(to, me).start()

    grid[...] = jnp.zeros_like(grid)
    block = taps.shape[0] // (kept + 2)
    for edge in (0, kept + 1):
        taps[edge * block : (edge + 1) * block, :] = jnp.zeros((block, lanes), taps.dtype)
    for edge in (0, reach_one + 1):
        first[edge * band : (edge + 1) * band, :] = jnp.zeros((band, lanes), first.dtype)
    for edge in (0, reach_two + 1):
        second[edge * band : (edge + 1) * band, :] = jnp.zeros((band, lanes), second.dtype)

    def select(shape, test):
        i = lax.broadcasted_iota(jnp.int32, shape, 0)
        m = lax.broadcasted_iota(jnp.int32, shape, 1)
        return test(i, m)

    for tap in range(block // slots):
        c, d = tap // 3, tap % 3

        def reaches(i, m):
            line = lax.div(m, columns) + c - 1
            spot = lax.rem(m, columns) + d - 1
            return (i == line * columns + spot) & (line >= 0) & (line < rows) & (spot >= 0) & (spot < columns)

        if tap < 9:
            move = select((lanes, lanes), reaches).astype(jnp.bfloat16)
        else:
            move = jnp.zeros((lanes, lanes), jnp.bfloat16)
        moves[:, tap * lanes : (tap + 1) * lanes] = move

    for load in loads[1:]:
        load.wait()
    count = wf_ref.shape[1]
    kernels = jnp.concatenate([wm_ref[...].reshape(depth * depth, count), wl_ref[...]], axis=0)
    height = kernels.shape[0]
    wide = 2 * lanes
    matching = select((height, wide), lambda i, m: lax.rem(i, depth) == lax.rem(m, depth))
    folding = select((32, height), lambda i, m: lax.div(m, depth) == i).astype(jnp.bfloat16)
    line_of = select((32, wide), lambda i, m: lax.div(lax.rem(m, band), depth))
    last_rows = [[] for _ in range(rows)]
    for tap in range(9):
        here = select(
            (count, wide),
            lambda i, m: (i == (lax.div(lax.rem(m, band), depth) * 3 + lax.div(m, band)) * 9 + tap)
            & (lax.rem(m, band) < 3 * depth)
            & (m < 3 * band),
        ).astype(jnp.bfloat16)
        picks = jnp.dot(kernels, here, preferred_element_type=jnp.float32)
        picks = jnp.where(matching, picks, 0.0).astype(jnp.bfloat16)
        folded = jnp.dot(folding, picks, preferred_element_type=jnp.float32)
        for turn in range(rows):
            shift = ((turn - 1) * depth) % wide
            moved = pltpu.roll(folded, shift, 1) if shift else folded
            moved = jnp.where((line_of >= turn - 1) & (line_of <= turn + 1), moved, 0.0)[:, : 3 * band]
            start = (turn * 9 + tap) * depth
            w2_ref[start : start + depth, :] = moved[:depth].astype(jnp.bfloat16)
            last_rows[turn].append(moved[depth : depth + 1])
    for turn in range(rows):
        last = jnp.concatenate(last_rows[turn] + [jnp.zeros((16 - 9, 3 * band), jnp.float32)], axis=0)
        w3_ref[turn * 16 : (turn + 1) * 16, :] = last.astype(jnp.bfloat16)

    for turn in range(rows):
        def uses(i, m):
            inside = lax.rem(m, block)
            a = lax.rem(inside, slots) - turn + 1
            tap = lax.div(inside, slots)
            return (i == 27 * a + 9 * lax.div(m, block) + tap) & (a >= 0) & (a < 3) & (tap < 9)

        here = select((count, 3 * block), uses).astype(jnp.bfloat16)
        packed = jnp.dot(wf_ref[...], here, preferred_element_type=jnp.float32)
        w1_ref[turn * depth : (turn + 1) * depth, :] = packed.astype(jnp.bfloat16)

    def masks(size):
        place = lax.broadcasted_iota(jnp.int32, (size, lanes), 1)
        line = lax.div(place, columns)
        spot = lax.rem(place, columns)
        lines = [((line + c - 1 >= 0) & (line + c - 1 < rows)).astype(jnp.float32) for c in range(3)]
        spots = [((spot + d - 1 >= 0) & (spot + d - 1 < columns)).astype(jnp.float32) for d in range(3)]
        return lines, spots

    def gathered(term_at, lines, spots):
        summed = None
        for c in range(3):
            inner = None
            for d in range(3):
                term = term_at(c * 3 + d)
                if d != 1:
                    term = pltpu.roll(term, (1 - d) % lanes, 1) * spots[d]
                inner = term if inner is None else inner + term
            if c != 1:
                inner = pltpu.roll(inner, ((1 - c) * columns) % lanes, 1) * lines[c]
            summed = inner if summed is None else summed + inner
        return jnp.maximum(summed, 0.0)

    for source in peers:
        hop(source, source).wait_recv()

    lot = lax.div(me, HALVES)
    side = lax.rem(me, HALVES)

    def pick(to, pair):
        return pltpu.make_async_remote_copy(
            src_ref=picked.at[to, pair], dst_ref=chosen.at[lot, row],
            send_sem=pick_send.at[to, pair], recv_sem=pick_recv.at[lot, row],
            device_id={"pair": to, "row": pair * HALVES + side}, device_id_type=MESH,
        )

    for to in routes + [me]:
        for pair in reversed(range(group_pairs)):
            index = to * group_pairs + pair
            source_image = held[slot_ref[src_ref[index]]]
            target_image = held[slot_ref[tgt_ref[index]]]
            picked[to, pair, 0] = source_image
            picked[to, pair, 1] = target_image
            if to is not me:
                pick(to, pair).start()
            else:
                @pl.when(pair * HALVES + side != row)
                def _():
                    pick(to, pair).start()

                @pl.when(pair * HALVES + side == row)
                def _():
                    chosen[lot, row, 0] = source_image
                    chosen[lot, row, 1] = target_image

    total = jnp.zeros((positions, positions), jnp.float32)
    for piece in range(groups // HALVES):
        source = piece * HALVES + half
        for turn in range(rows):
            @pl.when((source != me) | (row != turn))
            def _():
                pltpu.make_async_remote_copy(
                    src_ref=picked.at[0, 0], dst_ref=chosen.at[piece, turn],
                    send_sem=pick_send.at[0, 0], recv_sem=pick_recv.at[piece, turn],
                    device_id={"pair": source, "row": turn}, device_id_type=MESH,
                ).wait_recv()

        left = jnp.concatenate([chosen[piece, turn, 0] for turn in range(rows)], axis=0)
        right = jnp.concatenate([chosen[piece, turn, 1] for turn in range(rows)], axis=0)
        total = total + lax.dot_general(
            left, right, (((1,), (1,)), ((), ())), preferred_element_type=jnp.float32
        )
    partial[...] = total.reshape(partial.shape)
    off = columns - kept
    swap = pltpu.make_async_remote_copy(
        src_ref=partial.at[:, pl.ds(pl.multiple_of((1 - half) * off, off), kept)],
        dst_ref=other, send_sem=mate_sem.at[0], recv_sem=mate_sem.at[1],
        device_id={"row": row + 1 - 2 * half}, device_id_type=MESH,
    )
    swap.start()
    swap.wait()
    mine = partial[:, pl.ds(pl.multiple_of(half * off, off), kept), :]
    correlation = (mine + other[...]).astype(jnp.bfloat16).astype(jnp.float32)
    for turn in range(rows):
        grid[:, turn, :] = correlation[turn]
    cells = grid[...].reshape(kept * slots, lanes).astype(jnp.bfloat16)
    for pack in range(block // 16):
        shifted = jnp.dot(
            cells, moves[:, pack * 2 * lanes : (pack + 1) * 2 * lanes], preferred_element_type=jnp.float32
        )
        for j in range(kept):
            piece = shifted[j * slots : (j + 1) * slots]
            both = jnp.concatenate([piece[:, :lanes], piece[:, lanes:]], axis=0)
            start = (j + 1) * block + pack * 16
            taps[start : start + 16, :] = both.astype(jnp.bfloat16)

    def windows(ref, size, first_at):
        return jnp.concatenate(
            [ref[pl.ds(pl.multiple_of((first_at + n) * size, 16), 3 * size), :] for n in range(2)], axis=1
        )

    lead_one = half * (columns - reach_one - off)
    for t in range(0, reach_one, 2):
        product = jnp.dot(w1_ref[...], windows(taps, block, lead_one + t), preferred_element_type=jnp.float32)
        value = jnp.maximum(product, 0.0).astype(jnp.bfloat16)
        for n in range(2):
            first[(t + n + 1) * band : (t + n + 2) * band, :] = value[:, n * lanes : (n + 1) * lanes]

    lines, spots = masks(depth)
    for t in range(0, reach_two, 2):
        window = windows(first, band, 2 * half + t)
        product = jnp.dot(w2_ref[...], window, preferred_element_type=jnp.float32)
        for turn in range(rows):
            for n in range(2):
                value = gathered(
                    lambda tap: product[
                        (turn * 9 + tap) * depth : (turn * 9 + tap + 1) * depth, n * lanes : (n + 1) * lanes
                    ],
                    lines, spots,
                )
                start = (t + n + 1) * band + turn * depth
                second[start : start + depth, :] = value.astype(jnp.bfloat16)

    for t in range(0, share, 2):
        product = jnp.dot(w3_ref[...], windows(second, band, 2 * half + t), preferred_element_type=jnp.float32)
        for n in range(2):
            third[t + n] = product[:, n * lanes : (n + 1) * lanes]

    lines, spots = masks(share)
    peak = None
    for turn in range(rows):
        value = gathered(lambda tap: third[:, turn * 16 + tap, :], lines, spots)
        scores[turn] = value
        top = jnp.max(value, axis=0, keepdims=True)
        peak = top if peak is None else jnp.maximum(peak, top)
    peak = jnp.broadcast_to(peak, best.shape)
    best[...] = peak
    got_best[team, half] = peak

    def tell(turn):
        to = lax.rem(row + turn, rows)
        return pltpu.make_async_remote_copy(
            src_ref=best, dst_ref=got_best.at[team, half],
            send_sem=best_send.at[turn], recv_sem=best_recv.at[team, half],
            device_id={"row": to}, device_id_type=MESH,
        )

    def give(turn):
        to = lax.rem(row + turn, rows)
        return pltpu.make_async_remote_copy(
            src_ref=scores.at[to], dst_ref=got_scores.at[team, half],
            send_sem=score_send.at[turn], recv_sem=score_recv.at[team, half],
            device_id={"row": to}, device_id_type=MESH,
        )

    for turn in range(1, rows):
        give(turn).start()
        tell(turn).start()
    got_scores[team, half] = scores[row]

    for pair in range(group_pairs):
        for part in range(HALVES):
            origin = pair * HALVES + part

            @pl.when(origin != row)
            def _():
                pltpu.make_async_remote_copy(
                    src_ref=best, dst_ref=got_best.at[pair, part],
                    send_sem=best_send.at[1], recv_sem=best_recv.at[pair, part],
                    device_id={"row": origin}, device_id_type=MESH,
                ).wait_recv()
                pltpu.make_async_remote_copy(
                    src_ref=scores.at[0], dst_ref=got_scores.at[pair, part],
                    send_sem=score_send.at[1], recv_sem=score_recv.at[pair, part],
                    device_id={"row": origin}, device_id_type=MESH,
                ).wait_recv()

        source_best = got_best[pair, 0, 0:1, :]
        for part in range(1, HALVES):
            source_best = jnp.maximum(source_best, got_best[pair, part, 0:1, :])
        for part in range(HALVES):
            value = got_scores[pair, part]
            target_best = jnp.max(value, axis=-1, keepdims=True)
            o_ref[pair, 0, part * share : (part + 1) * share, :] = (
                value / (source_best + EPSILON) * (value / (target_best + EPSILON))
            ).astype(o_ref.dtype)

    for to in peers:
        hop(to, me).wait_send()
    for to in routes + [me]:
        for pair in range(group_pairs):
            if to is not me:
                pick(to, pair).wait_send()
            else:
                @pl.when(pair * HALVES + side != row)
                def _():
                    pick(to, pair).wait_send()
    for turn in range(1, rows):
        give(turn).wait_send()
        tell(turn).wait_send()


def spread(features, src_ids, tgt_ids, image_slot, w_first, w_mid, w_last):
    groups = lax.axis_size("pair")
    rows = lax.axis_size("row")
    local_images, _, columns, channels = features.shape
    chunk = channels // groups
    depth = w_mid.shape[1]
    group_pairs = src_ids.shape[0] // groups
    positions = rows * columns
    band = rows * depth
    share = columns // HALVES
    kept = share + 8
    slots = 8
    block = 10 * slots
    vmem = pl.BlockSpec(memory_space=pltpu.VMEM)
    dma = pltpu.SemaphoreType.DMA
    bf16, f32 = jnp.bfloat16, jnp.float32
    weights = (w_first.transpose(2, 1, 0)[0], w_mid.transpose(1, 2, 0), w_last.transpose(1, 2, 0)[0])
    result = pl.pallas_call(
        spread_kernel,
        out_shape=pltpu.VMEM((group_pairs, 1, columns, positions), f32),
        in_specs=[pl.BlockSpec(memory_space=pltpu.HBM)] * 7,
        out_specs=vmem,
        scratch_shapes=[
            pltpu.VMEM(features.shape, bf16),
            *(pltpu.VMEM(weight.shape, bf16) for weight in weights),
            *(pltpu.SMEM(ids.shape, jnp.int32) for ids in (src_ids, tgt_ids, image_slot)),
            dma((7,)),
            pltpu.VMEM((band, 3 * block), bf16),
            pltpu.VMEM((9 * band, 3 * band), bf16),
            pltpu.VMEM((rows * 16, 3 * band), bf16),
            pltpu.VMEM((positions, 10 * positions), bf16),
            pltpu.VMEM((groups, local_images, columns, chunk), bf16),
            pltpu.VMEM((groups * local_images, columns, chunk), bf16),
            pltpu.VMEM((groups, group_pairs, 2, columns, chunk), bf16),
            pltpu.VMEM((groups // HALVES, rows, 2, columns, chunk), bf16),
            pltpu.VMEM((rows, columns, positions), f32),
            pltpu.VMEM((rows, kept, positions), f32),
            pltpu.VMEM((kept, slots, positions), f32),
            pltpu.VMEM(((kept + 2) * block, positions), bf16),
            pltpu.VMEM(((share + 6) * band, positions), bf16),
            pltpu.VMEM(((share + 4) * band, positions), bf16),
            pltpu.VMEM((share, rows * 16, positions), f32),
            pltpu.VMEM((rows, share, positions), f32),
            pltpu.VMEM((8, positions), f32),
            pltpu.VMEM((group_pairs, HALVES, share, positions), f32),
            pltpu.VMEM((group_pairs, HALVES, 8, positions), f32),
            dma((groups,)), dma((groups,)),
            dma((groups, group_pairs)), dma((groups // HALVES, rows)),
            dma((2,)),
            dma((rows,)), dma((group_pairs, HALVES)),
            dma((rows,)), dma((group_pairs, HALVES)),
        ],
        compiler_params=pltpu.CompilerParams(
            collective_id=0, has_side_effects=True, vmem_limit_bytes=VMEM_LIMIT
        ),
    )(*(pltpu.with_memory_space_constraint(x, pltpu.HBM) for x in (features, *weights, src_ids, tgt_ids, image_slot)))
    return result.astype(bf16)


def program(features, src_ids, tgt_ids, image_slot, w_first, w_mid, w_last):
    groups = lax.axis_size("pair")
    rows = lax.axis_size("row")
    _, local_rows, columns, channels = features.shape
    fits = (
        local_rows == 1
        and groups % HALVES == 0
        and rows * groups == HALVES * src_ids.shape[0]
        and channels % (groups * 128) == 0
        and rows * columns == 128
        and columns == 32
        and rows == 2 * HALVES
        and w_mid.shape[1] == 16
    )
    run = spread if fits else local
    return run(features, src_ids, tgt_ids, image_slot, w_first, w_mid, w_last)


def solution(mesh):
    placed = (P("pair", "row", None, None), P(), P(), P(), P(), P(), P())
    return jax.shard_map(
        program, mesh=mesh, in_specs=placed, out_specs=P("pair", "row", None, None), check_vma=False
    )
```

```python
import jax
import jax.numpy as jnp
from jax import lax
from jax.experimental import pallas as pl
from jax.experimental.pallas import tpu as pltpu
from jax.sharding import PartitionSpec as P

WID = 32
HALVES = 2
HEAD = 4
VMEM_LIMIT = 16 << 20
MESH = pl.DeviceIdType.MESH


EPSILON = 1e-05
NORM_EPS = 1e-06


def with_halo(cells, sides, width):
    for axis, dim in sides:
        count = lax.axis_size(axis)
        ends = count - 1
        head = lax.slice_in_dim(cells, 0, width, axis=dim)
        tail = lax.slice_in_dim(cells, cells.shape[dim] - width, cells.shape[dim], axis=dim)
        cells = jnp.concatenate(
            [
                lax.ppermute(tail, axis, [(i, (i + 1) % count) for i in range(ends)]),
                cells,
                lax.ppermute(head, axis, [((i + 1) % count, i) for i in range(ends)]),
            ],
            axis=dim,
        )
    return cells


def slot_lookup(image_ids, image_slot):
    matches = image_ids[..., None] == jnp.arange(image_slot.shape[0], dtype=jnp.int32)
    return jnp.sum(jnp.where(matches, image_slot, 0), axis=-1)


def consensus_layer(tensor, weight, col_masks, is_last):
    group_pairs = tensor.shape[0]
    channels_in = tensor.shape[1]
    positions = tensor.shape[4]
    channels_out = weight.shape[1]
    rimmed = with_halo(tensor, (("row", 2),), 1)
    padded = jnp.pad(rimmed, ((0, 0), (0, 0), (0, 0), (1, 1), (0, 0)))
    matrix = (
        weight.reshape(9, 9, channels_out, channels_in)
        .transpose(1, 2, 0, 3)
        .reshape(9 * channels_out, 9 * channels_in)
    )
    results = []
    for member in range(group_pairs):
        stacked = jnp.stack(
            [padded[member, :, a, b : b + WID, :] for a in range(3) for b in range(3)]
        )
        product = jnp.dot(
            matrix,
            stacked.reshape(9 * channels_in, WID * positions),
            preferred_element_type=jnp.float32,
        )
        product = product.reshape(9, channels_out, WID, positions)
        summed = jnp.zeros((channels_out, WID, positions), jnp.float32)
        for c in range(3):
            for d in range(3):
                offset = (c - 1) * WID + (d - 1)
                widened = jnp.pad(product[c * 3 + d], ((0, 0), (0, 0), (WID + 1, WID + 1)))
                shifted = widened[:, :, WID + 1 + offset : WID + 1 + offset + positions]
                summed = summed + shifted * col_masks[d]
        outputs = [jax.nn.relu(summed)]
        results.append(jnp.stack(outputs, axis=1))
    result = jnp.stack(results, axis=0)
    if is_last:
        return result
    return result.astype(jnp.bfloat16)


def local(features, src_ids, tgt_ids, image_slot, w_first, w_mid, w_last):
    local_images, local_rows, columns, channels = features.shape
    block_rows = local_rows * columns
    flattened = features.reshape(local_images, block_rows, channels).astype(jnp.float32)
    scale = lax.rsqrt(jnp.sum(flattened * flattened, axis=-1, keepdims=True) + NORM_EPS)
    normed = (flattened * scale).astype(jnp.bfloat16)
    group_pairs = src_ids.shape[0] // lax.axis_size("pair")
    pair_index = lax.axis_index("pair")
    wanted_ids = jnp.stack([src_ids, tgt_ids], axis=1)
    own_ids = lax.dynamic_slice_in_dim(
        wanted_ids, pair_index * group_pairs, group_pairs, 0
    ).reshape(-1)
    needed = slot_lookup(own_ids, image_slot)
    shard_piece = lax.all_gather(normed, "pair", axis=0, tiled=True)
    length = shard_piece.shape[0]
    one_hot = (needed[:, None] == jnp.arange(length, dtype=jnp.int32)).astype(jnp.bfloat16)
    chosen = jnp.einsum("wk,krc->wrc", one_hot, shard_piece, preferred_element_type=jnp.float32)
    routed = chosen.astype(jnp.bfloat16)
    routed = routed.reshape(group_pairs, 2, block_rows, channels)
    sources = routed[:, 0]
    targets = routed[:, 1]
    correlation = jnp.einsum(
        "prc,ptc->prt",
        sources,
        lax.all_gather(targets, "row", axis=1, tiled=True),
        preferred_element_type=jnp.float32,
    )
    positions = correlation.shape[2]
    tensor = correlation.astype(jnp.bfloat16).reshape(
        group_pairs, 1, local_rows, columns, positions
    )
    target_col = jnp.arange(positions, dtype=jnp.int32) % WID
    col_masks = [
        ((target_col + d - 1 >= 0) & (target_col + d - 1 < WID)).astype(jnp.float32)
        for d in range(3)
    ]
    hidden_one = consensus_layer(tensor, w_first, col_masks, False)
    hidden_two = consensus_layer(hidden_one, w_mid, col_masks, False)
    consensus = consensus_layer(hidden_two, w_last, col_masks, True)[:, 0]
    target_best = jnp.max(consensus, axis=-1, keepdims=True)
    local_best = jnp.max(consensus, axis=(1, 2))
    source_best = lax.pmax(local_best, "row")
    matches = (
        consensus
        / (source_best[:, None, None, :] + EPSILON)
        * (consensus / (target_best + EPSILON))
    )
    return matches.astype(jnp.bfloat16)


def spread_kernel(
    x_any, wf_any, wm_any, wl_any, src_any, tgt_any, slot_any, o_ref,
    x_ref, wf_ref, wm_ref, wl_ref, src_ref, tgt_ref, slot_ref, load_sem,
    w1_ref, w2_ref, w3_ref, moves,
    parts, held, picked, chosen, partial, other, grid, taps, first, second, third,
    scores, best, got_scores, got_best,
    hop_send, hop_recv, pick_send, pick_recv, mate_sem, score_send, score_recv, best_send, best_recv,
):
    groups = lax.axis_size("pair")
    rows = lax.axis_size("row")
    me = lax.axis_index("pair")
    row = lax.axis_index("row")
    group_pairs = rows // HALVES
    team = lax.div(row, HALVES)
    half = lax.rem(row, HALVES)
    local_images, columns, chunk = parts.shape[1:]
    positions = rows * columns
    lanes = o_ref.shape[3]
    depth = wm_ref.shape[0]
    band = rows * depth
    slots = grid.shape[1]
    share = columns // HALVES
    kept = grid.shape[0]
    reach_one, reach_two = share + 4, share + 2

    loads = [
        pltpu.make_async_copy(source, target, load_sem.at[n])
        for n, (source, target) in enumerate(
            (
                (x_any, x_ref), (wf_any, wf_ref), (wm_any, wm_ref), (wl_any, wl_ref),
                (src_any, src_ref), (tgt_any, tgt_ref), (slot_any, slot_ref),
            )
        )
    ]
    loads[0].start()
    barrier = pltpu.get_barrier_semaphore()
    for step in range(1, groups):
        pl.semaphore_signal(
            barrier, inc=1, device_id={"pair": lax.rem(me + step, groups)}, device_id_type=MESH
        )
    for turn in range(1, rows):
        pl.semaphore_signal(
            barrier, inc=1, device_id={"row": lax.rem(row + turn, rows)}, device_id_type=MESH
        )

    low, high = me, groups - 1 - me
    near, gap = jnp.minimum(low, high), jnp.abs(high - low)

    def distant(step):
        single = jnp.where(high > low, groups - 1 - step, step)
        beyond = step - gap
        away = near - lax.div(beyond, 2)
        double = me + jnp.where(lax.rem(beyond, 2) == 0, away, -away)
        return jnp.where(step < gap, single, double)

    peers = [distant(step) for step in range(groups - 1)]
    routes = [jnp.where(k < me, k, k + 1) for k in range(groups - 1)]

    for load in loads[1:]:
        load.start()
    loads[0].wait()

    for image in range(local_images):
        cells = x_ref[image, 0].astype(jnp.float32)
        scale = lax.rsqrt(jnp.sum(cells * cells, axis=-1, keepdims=True) + NORM_EPS)
        normed = (cells * scale).astype(jnp.bfloat16)
        for piece in range(groups):
            parts[piece, image] = normed[:, piece * chunk : (piece + 1) * chunk]
    held[pl.ds(me * local_images, local_images)] = parts[me]
    pl.semaphore_wait(barrier, groups + rows - 2)

    def arrived(where, semaphore):
        pltpu.make_async_remote_copy(
            src_ref=where, dst_ref=where, send_sem=semaphore, recv_sem=semaphore,
            device_id={"row": row}, device_id_type=MESH,
        ).wait_recv()

    def sent(where, semaphore):
        pltpu.make_async_remote_copy(
            src_ref=where, dst_ref=where, send_sem=semaphore, recv_sem=semaphore,
            device_id={"row": row}, device_id_type=MESH,
        ).wait_send()

    def hop(peer, slot):
        return pltpu.make_async_remote_copy(
            src_ref=parts.at[peer],
            dst_ref=held.at[pl.ds(slot * local_images, local_images)],
            send_sem=hop_send.at[0], recv_sem=hop_recv.at[0],
            device_id={"pair": peer}, device_id_type=MESH,
        )

    for to in peers:
        hop(to, me).start()

    grid[...] = jnp.zeros_like(grid)
    block = taps.shape[0] // (kept + 2)
    for edge in (0, kept + 1):
        taps[edge * block : (edge + 1) * block, :] = jnp.zeros((block, lanes), taps.dtype)
    for edge in (0, reach_one + 1):
        first[edge * band : (edge + 1) * band, :] = jnp.zeros((band, lanes), first.dtype)
    for edge in (0, reach_two + 1):
        second[edge * band : (edge + 1) * band, :] = jnp.zeros((band, lanes), second.dtype)

    def select(shape, test):
        i = lax.broadcasted_iota(jnp.int32, shape, 0)
        m = lax.broadcasted_iota(jnp.int32, shape, 1)
        return test(i, m)

    for tap in range(block // slots):
        c, d = tap // 3, tap % 3

        def reaches(i, m):
            line = lax.div(m, columns) + c - 1
            spot = lax.rem(m, columns) + d - 1
            return (i == line * columns + spot) & (line >= 0) & (line < rows) & (spot >= 0) & (spot < columns)

        if tap < 9:
            move = select((lanes, lanes), reaches).astype(jnp.bfloat16)
        else:
            move = jnp.zeros((lanes, lanes), jnp.bfloat16)
        moves[:, tap * lanes : (tap + 1) * lanes] = move

    for load in loads[1:]:
        load.wait()
    count = wf_ref.shape[1]
    kernels = jnp.concatenate([wm_ref[...].reshape(depth * depth, count), wl_ref[...]], axis=0)
    height = kernels.shape[0]
    wide = 2 * lanes
    matching = select((height, wide), lambda i, m: lax.rem(i, depth) == lax.rem(m, depth))
    folding = select((32, height), lambda i, m: lax.div(m, depth) == i).astype(jnp.bfloat16)
    line_of = select((32, wide), lambda i, m: lax.div(lax.rem(m, band), depth))
    last_rows = [[] for _ in range(rows)]
    for tap in range(9):
        here = select(
            (count, wide),
            lambda i, m: (i == (lax.div(lax.rem(m, band), depth) * 3 + lax.div(m, band)) * 9 + tap)
            & (lax.rem(m, band) < 3 * depth)
            & (m < 3 * band),
        ).astype(jnp.bfloat16)
        picks = jnp.dot(kernels, here, preferred_element_type=jnp.float32)
        picks = jnp.where(matching, picks, 0.0).astype(jnp.bfloat16)
        folded = jnp.dot(folding, picks, preferred_element_type=jnp.float32)
        for turn in range(rows):
            shift = ((turn - 1) * depth) % wide
            moved = pltpu.roll(folded, shift, 1) if shift else folded
            moved = jnp.where((line_of >= turn - 1) & (line_of <= turn + 1), moved, 0.0)[:, : 3 * band]
            start = (turn * 9 + tap) * depth
            w2_ref[start : start + depth, :] = moved[:depth].astype(jnp.bfloat16)
            last_rows[turn].append(moved[depth : depth + 1])
    for turn in range(rows):
        last = jnp.concatenate(last_rows[turn] + [jnp.zeros((16 - 9, 3 * band), jnp.float32)], axis=0)
        w3_ref[turn * 16 : (turn + 1) * 16, :] = last.astype(jnp.bfloat16)

    for turn in range(rows):
        def uses(i, m):
            inside = lax.rem(m, block)
            a = lax.rem(inside, slots) - turn + 1
            tap = lax.div(inside, slots)
            return (i == 27 * a + 9 * lax.div(m, block) + tap) & (a >= 0) & (a < 3) & (tap < 9)

        here = select((count, 3 * block), uses).astype(jnp.bfloat16)
        packed = jnp.dot(wf_ref[...], here, preferred_element_type=jnp.float32)
        w1_ref[turn * depth : (turn + 1) * depth, :] = packed.astype(jnp.bfloat16)

    def masks(size):
        place = lax.broadcasted_iota(jnp.int32, (size, lanes), 1)
        line = lax.div(place, columns)
        spot = lax.rem(place, columns)
        lines = [((line + c - 1 >= 0) & (line + c - 1 < rows)).astype(jnp.float32) for c in range(3)]
        spots = [((spot + d - 1 >= 0) & (spot + d - 1 < columns)).astype(jnp.float32) for d in range(3)]
        return lines, spots

    def gathered(term_at, lines, spots):
        summed = None
        for c in range(3):
            inner = None
            for d in range(3):
                term = term_at(c * 3 + d)
                if d != 1:
                    term = pltpu.roll(term, (1 - d) % lanes, 1) * spots[d]
                inner = term if inner is None else inner + term
            if c != 1:
                inner = pltpu.roll(inner, ((1 - c) * columns) % lanes, 1) * lines[c]
            summed = inner if summed is None else summed + inner
        return jnp.maximum(summed, 0.0)

    wanted = {}
    for step, to in enumerate(routes + [me]):
        for pair in range(group_pairs):
            index = to * group_pairs + pair
            wanted[step, pair] = slot_ref[src_ref[index]], slot_ref[tgt_ref[index]]
    arrived(held.at[pl.ds(0, (groups - 1) * local_images)], hop_recv.at[0])

    lot = lax.div(me, HALVES)
    side = lax.rem(me, HALVES)

    def pick(to, pair):
        return pltpu.make_async_remote_copy(
            src_ref=picked.at[to, pair], dst_ref=chosen.at[lot, row],
            send_sem=pick_send.at[0], recv_sem=pick_recv.at[lot],
            device_id={"pair": to, "row": pair * HALVES + side}, device_id_type=MESH,
        )

    def gather_pick(step, to, pair):
        source_slot, target_slot = wanted[step, pair]
        source_image = held[source_slot]
        target_image = held[target_slot]
        picked[to, pair, 0] = source_image
        picked[to, pair, 1] = target_image
        if to is me:
            @pl.when(pair * HALVES + side == row)
            def _():
                pltpu.make_async_copy(picked.at[me, pair], chosen.at[lot, row], pick_recv.at[lot]).start()

    def send_pick(to, pair):
        if to is not me:
            pick(to, pair).start()
        else:
            @pl.when(pair * HALVES + side != row)
            def _():
                pick(to, pair).start()

    turns = [(step, to, pair) for step, to in enumerate(routes + [me]) for pair in reversed(range(group_pairs))]
    for part in (turns[:HEAD], turns[HEAD:]):
        for step, to, pair in part:
            gather_pick(step, to, pair)
        for step, to, pair in part:
            send_pick(to, pair)

    total = jnp.zeros((positions, positions), jnp.float32)
    for piece in range(groups // HALVES):
        arrived(chosen.at[piece], pick_recv.at[piece])
        left = jnp.concatenate([chosen[piece, turn, 0] for turn in range(rows)], axis=0)
        right = jnp.concatenate([chosen[piece, turn, 1] for turn in range(rows)], axis=0)
        total = total + lax.dot_general(
            left, right, (((1,), (1,)), ((), ())), preferred_element_type=jnp.float32
        )
    partial[...] = total.reshape(partial.shape)
    off = columns - kept
    swap = pltpu.make_async_remote_copy(
        src_ref=partial.at[:, pl.ds(pl.multiple_of((1 - half) * off, off), kept)],
        dst_ref=other, send_sem=mate_sem.at[0], recv_sem=mate_sem.at[1],
        device_id={"row": row + 1 - 2 * half}, device_id_type=MESH,
    )
    swap.start()
    swap.wait()
    mine = partial[:, pl.ds(pl.multiple_of(half * off, off), kept), :]
    correlation = (mine + other[...]).astype(jnp.bfloat16).astype(jnp.float32)
    for turn in range(rows):
        grid[:, turn, :] = correlation[turn]
    cells = grid[...].reshape(kept * slots, lanes).astype(jnp.bfloat16)
    for pack in range(block // 16):
        shifted = jnp.dot(
            cells, moves[:, pack * 2 * lanes : (pack + 1) * 2 * lanes], preferred_element_type=jnp.float32
        )
        for j in range(kept):
            piece = shifted[j * slots : (j + 1) * slots]
            both = jnp.concatenate([piece[:, :lanes], piece[:, lanes:]], axis=0)
            start = (j + 1) * block + pack * 16
            taps[start : start + 16, :] = both.astype(jnp.bfloat16)

    def windows(ref, size, first_at):
        return jnp.concatenate(
            [ref[pl.ds(pl.multiple_of((first_at + n) * size, 16), 3 * size), :] for n in range(2)], axis=1
        )

    lead_one = half * (columns - reach_one - off)
    for t in range(0, reach_one, 2):
        product = jnp.dot(w1_ref[...], windows(taps, block, lead_one + t), preferred_element_type=jnp.float32)
        value = jnp.maximum(product, 0.0).astype(jnp.bfloat16)
        for n in range(2):
            first[(t + n + 1) * band : (t + n + 2) * band, :] = value[:, n * lanes : (n + 1) * lanes]

    lines, spots = masks(depth)
    for t in range(0, reach_two, 2):
        window = windows(first, band, 2 * half + t)
        product = jnp.dot(w2_ref[...], window, preferred_element_type=jnp.float32)
        for turn in range(rows):
            for n in range(2):
                value = gathered(
                    lambda tap: product[
                        (turn * 9 + tap) * depth : (turn * 9 + tap + 1) * depth, n * lanes : (n + 1) * lanes
                    ],
                    lines, spots,
                )
                start = (t + n + 1) * band + turn * depth
                second[start : start + depth, :] = value.astype(jnp.bfloat16)

    for t in range(0, share, 2):
        product = jnp.dot(w3_ref[...], windows(second, band, 2 * half + t), preferred_element_type=jnp.float32)
        for n in range(2):
            third[t + n] = product[:, n * lanes : (n + 1) * lanes]

    lines, spots = masks(share)
    peak = None
    for turn in range(rows):
        value = gathered(lambda tap: third[:, turn * 16 + tap, :], lines, spots)
        scores[turn] = value
        top = jnp.max(value, axis=0, keepdims=True)
        peak = top if peak is None else jnp.maximum(peak, top)
    peak = jnp.broadcast_to(peak, best.shape)
    best[...] = peak
    got_best[row] = peak

    def tell(to):
        return pltpu.make_async_remote_copy(
            src_ref=best, dst_ref=got_best.at[row],
            send_sem=best_send.at[0], recv_sem=best_recv.at[0],
            device_id={"row": to}, device_id_type=MESH,
        )

    def give(to):
        return pltpu.make_async_remote_copy(
            src_ref=scores.at[to], dst_ref=got_scores.at[row],
            send_sem=score_send.at[0], recv_sem=score_recv.at[0],
            device_id={"row": to}, device_id_type=MESH,
        )

    others = [(1 - team) * HALVES + n for n in range(HALVES)] + [row + 1 - 2 * half]
    for to in others:
        give(to).start()
        tell(to).start()
    got_scores[row] = scores[row]

    sent(held.at[pl.ds(0, (groups - 1) * local_images)], hop_send.at[0])
    sent(picked.at[pl.ds(0, groups - 1)], pick_send.at[0])
    for pair in range(group_pairs):
        @pl.when(pair * HALVES + side != row)
        def _():
            sent(picked.at[0, 0], pick_send.at[0])

    arrived(got_scores.at[pl.ds(0, rows - 1)], score_recv.at[0])
    arrived(got_best.at[pl.ds(0, rows - 1)], best_recv.at[0])
    for pair in range(group_pairs):
        source_best = got_best[pair * HALVES, 0:1, :]
        for part in range(1, HALVES):
            source_best = jnp.maximum(source_best, got_best[pair * HALVES + part, 0:1, :])
        for part in range(HALVES):
            value = got_scores[pair * HALVES + part]
            target_best = jnp.max(value, axis=-1, keepdims=True)
            o_ref[pair, 0, part * share : (part + 1) * share, :] = (
                value / (source_best + EPSILON) * (value / (target_best + EPSILON))
            ).astype(o_ref.dtype)

    sent(got_scores.at[pl.ds(0, rows - 1)], score_send.at[0])
    sent(got_best.at[pl.ds(0, rows - 1)], best_send.at[0])


def spread(features, src_ids, tgt_ids, image_slot, w_first, w_mid, w_last):
    groups = lax.axis_size("pair")
    rows = lax.axis_size("row")
    local_images, _, columns, channels = features.shape
    chunk = channels // groups
    depth = w_mid.shape[1]
    group_pairs = src_ids.shape[0] // groups
    positions = rows * columns
    band = rows * depth
    share = columns // HALVES
    kept = share + 8
    slots = 8
    block = 10 * slots
    vmem = pl.BlockSpec(memory_space=pltpu.VMEM)
    dma = pltpu.SemaphoreType.DMA
    bf16, f32 = jnp.bfloat16, jnp.float32
    weights = (w_first.transpose(2, 1, 0)[0], w_mid.transpose(1, 2, 0), w_last.transpose(1, 2, 0)[0])
    result = pl.pallas_call(
        spread_kernel,
        out_shape=pltpu.VMEM((group_pairs, 1, columns, positions), f32),
        in_specs=[pl.BlockSpec(memory_space=pltpu.HBM)] * 7,
        out_specs=vmem,
        scratch_shapes=[
            pltpu.VMEM(features.shape, bf16),
            *(pltpu.VMEM(weight.shape, bf16) for weight in weights),
            *(pltpu.SMEM(ids.shape, jnp.int32) for ids in (src_ids, tgt_ids, image_slot)),
            dma((7,)),
            pltpu.VMEM((band, 3 * block), bf16),
            pltpu.VMEM((9 * band, 3 * band), bf16),
            pltpu.VMEM((rows * 16, 3 * band), bf16),
            pltpu.VMEM((positions, 10 * positions), bf16),
            pltpu.VMEM((groups, local_images, columns, chunk), bf16),
            pltpu.VMEM((groups * local_images, columns, chunk), bf16),
            pltpu.VMEM((groups, group_pairs, 2, columns, chunk), bf16),
            pltpu.VMEM((groups // HALVES, rows, 2, columns, chunk), bf16),
            pltpu.VMEM((rows, columns, positions), f32),
            pltpu.VMEM((rows, kept, positions), f32),
            pltpu.VMEM((kept, slots, positions), f32),
            pltpu.VMEM(((kept + 2) * block, positions), bf16),
            pltpu.VMEM(((share + 6) * band, positions), bf16),
            pltpu.VMEM(((share + 4) * band, positions), bf16),
            pltpu.VMEM((share, rows * 16, positions), f32),
            pltpu.VMEM((rows, share, positions), f32),
            pltpu.VMEM((8, positions), f32),
            pltpu.VMEM((rows, share, positions), f32),
            pltpu.VMEM((rows, 8, positions), f32),
            dma((1,)), dma((1,)),
            dma((1,)), dma((groups // HALVES,)),
            dma((2,)),
            dma((1,)), dma((1,)),
            dma((1,)), dma((1,)),
        ],
        compiler_params=pltpu.CompilerParams(
            collective_id=0, has_side_effects=True, vmem_limit_bytes=VMEM_LIMIT
        ),
    )(*(pltpu.with_memory_space_constraint(x, pltpu.HBM) for x in (features, *weights, src_ids, tgt_ids, image_slot)))
    return result.astype(bf16)


def program(features, src_ids, tgt_ids, image_slot, w_first, w_mid, w_last):
    groups = lax.axis_size("pair")
    rows = lax.axis_size("row")
    _, local_rows, columns, channels = features.shape
    fits = (
        local_rows == 1
        and groups % HALVES == 0
        and rows * groups == HALVES * src_ids.shape[0]
        and channels % (groups * 128) == 0
        and rows * columns == 128
        and columns == 32
        and rows == 2 * HALVES
        and w_mid.shape[1] == 16
    )
    run = spread if fits else local
    return run(features, src_ids, tgt_ids, image_slot, w_first, w_mid, w_last)


def solution(mesh):
    placed = (P("pair", "row", None, None), P(), P(), P(), P(), P(), P())
    return jax.shard_map(
        program, mesh=mesh, in_specs=placed, out_specs=P("pair", "row", None, None), check_vma=False
    )
```

```python
import jax
import jax.numpy as jnp
from jax import lax
from jax.experimental import pallas as pl
from jax.experimental.pallas import tpu as pltpu
from jax.sharding import PartitionSpec as P

WID = 32
HALVES = 2
HEAD = 2
VMEM_LIMIT = 16 << 20
MESH = pl.DeviceIdType.MESH


EPSILON = 1e-05
NORM_EPS = 1e-06


def with_halo(cells, sides, width):
    for axis, dim in sides:
        count = lax.axis_size(axis)
        ends = count - 1
        head = lax.slice_in_dim(cells, 0, width, axis=dim)
        tail = lax.slice_in_dim(cells, cells.shape[dim] - width, cells.shape[dim], axis=dim)
        cells = jnp.concatenate(
            [
                lax.ppermute(tail, axis, [(i, (i + 1) % count) for i in range(ends)]),
                cells,
                lax.ppermute(head, axis, [((i + 1) % count, i) for i in range(ends)]),
            ],
            axis=dim,
        )
    return cells


def slot_lookup(image_ids, image_slot):
    matches = image_ids[..., None] == jnp.arange(image_slot.shape[0], dtype=jnp.int32)
    return jnp.sum(jnp.where(matches, image_slot, 0), axis=-1)


def consensus_layer(tensor, weight, col_masks, is_last):
    group_pairs = tensor.shape[0]
    channels_in = tensor.shape[1]
    positions = tensor.shape[4]
    channels_out = weight.shape[1]
    rimmed = with_halo(tensor, (("row", 2),), 1)
    padded = jnp.pad(rimmed, ((0, 0), (0, 0), (0, 0), (1, 1), (0, 0)))
    matrix = (
        weight.reshape(9, 9, channels_out, channels_in)
        .transpose(1, 2, 0, 3)
        .reshape(9 * channels_out, 9 * channels_in)
    )
    results = []
    for member in range(group_pairs):
        stacked = jnp.stack(
            [padded[member, :, a, b : b + WID, :] for a in range(3) for b in range(3)]
        )
        product = jnp.dot(
            matrix,
            stacked.reshape(9 * channels_in, WID * positions),
            preferred_element_type=jnp.float32,
        )
        product = product.reshape(9, channels_out, WID, positions)
        summed = jnp.zeros((channels_out, WID, positions), jnp.float32)
        for c in range(3):
            for d in range(3):
                offset = (c - 1) * WID + (d - 1)
                widened = jnp.pad(product[c * 3 + d], ((0, 0), (0, 0), (WID + 1, WID + 1)))
                shifted = widened[:, :, WID + 1 + offset : WID + 1 + offset + positions]
                summed = summed + shifted * col_masks[d]
        outputs = [jax.nn.relu(summed)]
        results.append(jnp.stack(outputs, axis=1))
    result = jnp.stack(results, axis=0)
    if is_last:
        return result
    return result.astype(jnp.bfloat16)


def local(features, src_ids, tgt_ids, image_slot, w_first, w_mid, w_last):
    local_images, local_rows, columns, channels = features.shape
    block_rows = local_rows * columns
    flattened = features.reshape(local_images, block_rows, channels).astype(jnp.float32)
    scale = lax.rsqrt(jnp.sum(flattened * flattened, axis=-1, keepdims=True) + NORM_EPS)
    normed = (flattened * scale).astype(jnp.bfloat16)
    group_pairs = src_ids.shape[0] // lax.axis_size("pair")
    pair_index = lax.axis_index("pair")
    wanted_ids = jnp.stack([src_ids, tgt_ids], axis=1)
    own_ids = lax.dynamic_slice_in_dim(
        wanted_ids, pair_index * group_pairs, group_pairs, 0
    ).reshape(-1)
    needed = slot_lookup(own_ids, image_slot)
    shard_piece = lax.all_gather(normed, "pair", axis=0, tiled=True)
    length = shard_piece.shape[0]
    one_hot = (needed[:, None] == jnp.arange(length, dtype=jnp.int32)).astype(jnp.bfloat16)
    chosen = jnp.einsum("wk,krc->wrc", one_hot, shard_piece, preferred_element_type=jnp.float32)
    routed = chosen.astype(jnp.bfloat16)
    routed = routed.reshape(group_pairs, 2, block_rows, channels)
    sources = routed[:, 0]
    targets = routed[:, 1]
    correlation = jnp.einsum(
        "prc,ptc->prt",
        sources,
        lax.all_gather(targets, "row", axis=1, tiled=True),
        preferred_element_type=jnp.float32,
    )
    positions = correlation.shape[2]
    tensor = correlation.astype(jnp.bfloat16).reshape(
        group_pairs, 1, local_rows, columns, positions
    )
    target_col = jnp.arange(positions, dtype=jnp.int32) % WID
    col_masks = [
        ((target_col + d - 1 >= 0) & (target_col + d - 1 < WID)).astype(jnp.float32)
        for d in range(3)
    ]
    hidden_one = consensus_layer(tensor, w_first, col_masks, False)
    hidden_two = consensus_layer(hidden_one, w_mid, col_masks, False)
    consensus = consensus_layer(hidden_two, w_last, col_masks, True)[:, 0]
    target_best = jnp.max(consensus, axis=-1, keepdims=True)
    local_best = jnp.max(consensus, axis=(1, 2))
    source_best = lax.pmax(local_best, "row")
    matches = (
        consensus
        / (source_best[:, None, None, :] + EPSILON)
        * (consensus / (target_best + EPSILON))
    )
    return matches.astype(jnp.bfloat16)


def spread_kernel(
    x_any, wf_any, wm_any, wl_any, src_any, tgt_any, slot_any, o_ref,
    x_ref, wf_ref, wm_ref, wl_ref, src_ref, tgt_ref, slot_ref, load_sem,
    w1_ref, w2_ref, w3_ref, moves,
    parts, held, picked, chosen, partial, other, grid, taps, first, second, third,
    scores, got_scores,
    hop_send, hop_recv, pick_send, pick_recv, mate_sem, score_send, score_recv,
):
    groups = lax.axis_size("pair")
    rows = lax.axis_size("row")
    me = lax.axis_index("pair")
    row = lax.axis_index("row")
    group_pairs = rows // HALVES
    team = lax.div(row, HALVES)
    half = lax.rem(row, HALVES)
    local_images, columns, chunk = parts.shape[1:]
    positions = rows * columns
    lanes = o_ref.shape[3]
    depth = wm_ref.shape[0]
    band = rows * depth
    slots = grid.shape[1]
    share = columns // HALVES
    kept = grid.shape[0]
    reach_one, reach_two = share + 4, share + 2

    loads = [
        pltpu.make_async_copy(source, target, load_sem.at[n])
        for n, (source, target) in enumerate(
            (
                (x_any, x_ref), (wf_any, wf_ref), (wm_any, wm_ref), (wl_any, wl_ref),
                (src_any, src_ref), (tgt_any, tgt_ref), (slot_any, slot_ref),
            )
        )
    ]
    loads[0].start()
    barrier = pltpu.get_barrier_semaphore()
    for step in range(1, groups):
        pl.semaphore_signal(
            barrier, inc=1, device_id={"pair": lax.rem(me + step, groups)}, device_id_type=MESH
        )
    for turn in range(1, rows):
        pl.semaphore_signal(
            barrier, inc=1, device_id={"row": lax.rem(row + turn, rows)}, device_id_type=MESH
        )

    low, high = me, groups - 1 - me
    near, gap = jnp.minimum(low, high), jnp.abs(high - low)

    def distant(step):
        single = jnp.where(high > low, groups - 1 - step, step)
        beyond = step - gap
        away = near - lax.div(beyond, 2)
        double = me + jnp.where(lax.rem(beyond, 2) == 0, away, -away)
        return jnp.where(step < gap, single, double)

    peers = [distant(step) for step in range(groups - 1)]
    routes = [jnp.where(k < me, k, k + 1) for k in range(groups - 1)]

    for load in loads[1:]:
        load.start()
    loads[0].wait()

    for image in range(local_images):
        cells = x_ref[image, 0].astype(jnp.float32)
        scale = lax.rsqrt(jnp.sum(cells * cells, axis=-1, keepdims=True) + NORM_EPS)
        normed = (cells * scale).astype(jnp.bfloat16)
        for piece in range(groups):
            parts[piece, image] = normed[:, piece * chunk : (piece + 1) * chunk]
    held[pl.ds(me * local_images, local_images)] = parts[me]
    pl.semaphore_wait(barrier, groups + rows - 2)

    def arrived(where, semaphore):
        pltpu.make_async_remote_copy(
            src_ref=where, dst_ref=where, send_sem=semaphore, recv_sem=semaphore,
            device_id={"row": row}, device_id_type=MESH,
        ).wait_recv()

    def sent(where, semaphore):
        pltpu.make_async_remote_copy(
            src_ref=where, dst_ref=where, send_sem=semaphore, recv_sem=semaphore,
            device_id={"row": row}, device_id_type=MESH,
        ).wait_send()

    def hop(peer, slot):
        return pltpu.make_async_remote_copy(
            src_ref=parts.at[peer],
            dst_ref=held.at[pl.ds(slot * local_images, local_images)],
            send_sem=hop_send.at[0], recv_sem=hop_recv.at[0],
            device_id={"pair": peer}, device_id_type=MESH,
        )

    for to in peers:
        hop(to, me).start()

    grid[...] = jnp.zeros_like(grid)
    block = taps.shape[0] // (kept + 2)
    for edge in (0, kept + 1):
        taps[edge * block : (edge + 1) * block, :] = jnp.zeros((block, lanes), taps.dtype)
    for edge in (0, reach_one + 1):
        first[edge * band : (edge + 1) * band, :] = jnp.zeros((band, lanes), first.dtype)
    for edge in (0, reach_two + 1):
        second[edge * band : (edge + 1) * band, :] = jnp.zeros((band, lanes), second.dtype)

    def select(shape, test):
        i = lax.broadcasted_iota(jnp.int32, shape, 0)
        m = lax.broadcasted_iota(jnp.int32, shape, 1)
        return test(i, m)

    for tap in range(block // slots):
        c, d = tap // 3, tap % 3

        def reaches(i, m):
            line = lax.div(m, columns) + c - 1
            spot = lax.rem(m, columns) + d - 1
            return (i == line * columns + spot) & (line >= 0) & (line < rows) & (spot >= 0) & (spot < columns)

        if tap < 9:
            move = select((lanes, lanes), reaches).astype(jnp.bfloat16)
        else:
            move = jnp.zeros((lanes, lanes), jnp.bfloat16)
        moves[:, tap * lanes : (tap + 1) * lanes] = move

    for load in loads[1:]:
        load.wait()
    count = wf_ref.shape[1]
    kernels = jnp.concatenate([wm_ref[...].reshape(depth * depth, count), wl_ref[...]], axis=0)
    height = kernels.shape[0]
    wide = 2 * lanes
    matching = select((height, wide), lambda i, m: lax.rem(i, depth) == lax.rem(m, depth))
    folding = select((32, height), lambda i, m: lax.div(m, depth) == i).astype(jnp.bfloat16)
    line_of = select((32, wide), lambda i, m: lax.div(lax.rem(m, band), depth))
    last_rows = [[] for _ in range(rows)]
    for tap in range(9):
        here = select(
            (count, wide),
            lambda i, m: (i == (lax.div(lax.rem(m, band), depth) * 3 + lax.div(m, band)) * 9 + tap)
            & (lax.rem(m, band) < 3 * depth)
            & (m < 3 * band),
        ).astype(jnp.bfloat16)
        picks = jnp.dot(kernels, here, preferred_element_type=jnp.float32)
        picks = jnp.where(matching, picks, 0.0).astype(jnp.bfloat16)
        folded = jnp.dot(folding, picks, preferred_element_type=jnp.float32)
        for turn in range(rows):
            shift = ((turn - 1) * depth) % wide
            moved = pltpu.roll(folded, shift, 1) if shift else folded
            moved = jnp.where((line_of >= turn - 1) & (line_of <= turn + 1), moved, 0.0)[:, : 3 * band]
            start = (turn * 9 + tap) * depth
            w2_ref[start : start + depth, :] = moved[:depth].astype(jnp.bfloat16)
            last_rows[turn].append(moved[depth : depth + 1])
    for turn in range(rows):
        last = jnp.concatenate(last_rows[turn] + [jnp.zeros((16 - 9, 3 * band), jnp.float32)], axis=0)
        w3_ref[turn * 16 : (turn + 1) * 16, :] = last.astype(jnp.bfloat16)

    for turn in range(rows):
        def uses(i, m):
            inside = lax.rem(m, block)
            a = lax.rem(inside, slots) - turn + 1
            tap = lax.div(inside, slots)
            return (i == 27 * a + 9 * lax.div(m, block) + tap) & (a >= 0) & (a < 3) & (tap < 9)

        here = select((count, 3 * block), uses).astype(jnp.bfloat16)
        packed = jnp.dot(wf_ref[...], here, preferred_element_type=jnp.float32)
        w1_ref[turn * depth : (turn + 1) * depth, :] = packed.astype(jnp.bfloat16)

    def masks(size):
        place = lax.broadcasted_iota(jnp.int32, (size, lanes), 1)
        line = lax.div(place, columns)
        spot = lax.rem(place, columns)
        lines = [((line + c - 1 >= 0) & (line + c - 1 < rows)).astype(jnp.float32) for c in range(3)]
        spots = [((spot + d - 1 >= 0) & (spot + d - 1 < columns)).astype(jnp.float32) for d in range(3)]
        return lines, spots

    def gathered(term_at, lines, spots):
        summed = None
        for c in range(3):
            inner = None
            for d in range(3):
                term = term_at(c * 3 + d)
                if d != 1:
                    term = pltpu.roll(term, (1 - d) % lanes, 1) * spots[d]
                inner = term if inner is None else inner + term
            if c != 1:
                inner = pltpu.roll(inner, ((1 - c) * columns) % lanes, 1) * lines[c]
            summed = inner if summed is None else summed + inner
        return jnp.maximum(summed, 0.0)

    wanted = {}
    for step, to in enumerate(routes + [me]):
        for pair in range(group_pairs):
            index = to * group_pairs + pair
            wanted[step, pair] = slot_ref[src_ref[index]], slot_ref[tgt_ref[index]]
    arrived(held.at[pl.ds(0, (groups - 1) * local_images)], hop_recv.at[0])

    lot = lax.div(me, HALVES)
    side = lax.rem(me, HALVES)

    def pick(to, pair):
        return pltpu.make_async_remote_copy(
            src_ref=picked.at[to, pair], dst_ref=chosen.at[lot, row],
            send_sem=pick_send.at[0], recv_sem=pick_recv.at[lot],
            device_id={"pair": to, "row": pair * HALVES + side}, device_id_type=MESH,
        )

    def gather_pick(step, to, pair):
        source_slot, target_slot = wanted[step, pair]
        source_image = held[source_slot]
        target_image = held[target_slot]
        picked[to, pair, 0] = source_image
        picked[to, pair, 1] = target_image
        if to is me:
            @pl.when(pair * HALVES + side == row)
            def _():
                pltpu.make_async_copy(picked.at[me, pair], chosen.at[lot, row], pick_recv.at[lot]).start()

    def send_pick(to, pair):
        if to is not me:
            pick(to, pair).start()
        else:
            @pl.when(pair * HALVES + side != row)
            def _():
                pick(to, pair).start()

    turns = [(step, to, pair) for step, to in enumerate(routes + [me]) for pair in reversed(range(group_pairs))]
    for part in (turns[:HEAD], turns[HEAD:]):
        for step, to, pair in part:
            gather_pick(step, to, pair)
        for step, to, pair in part:
            send_pick(to, pair)

    total = jnp.zeros((positions, positions), jnp.float32)
    teams = groups // HALVES
    toward = jnp.where(lot < teams // 2, 1, -1)
    for step in range(teams):
        piece = lax.rem(lot + toward * step + teams, teams)
        arrived(chosen.at[piece], pick_recv.at[piece])
        left = jnp.concatenate([chosen[piece, turn, 0] for turn in range(rows)], axis=0)
        right = jnp.concatenate([chosen[piece, turn, 1] for turn in range(rows)], axis=0)
        total = total + lax.dot_general(
            left, right, (((1,), (1,)), ((), ())), preferred_element_type=jnp.float32
        )
    partial[...] = total.reshape(partial.shape)
    off = columns - kept
    swap = pltpu.make_async_remote_copy(
        src_ref=partial.at[:, pl.ds(pl.multiple_of((1 - half) * off, off), kept)],
        dst_ref=other, send_sem=mate_sem.at[0], recv_sem=mate_sem.at[1],
        device_id={"row": row + 1 - 2 * half}, device_id_type=MESH,
    )
    swap.start()
    swap.wait()
    mine = partial[:, pl.ds(pl.multiple_of(half * off, off), kept), :]
    correlation = (mine + other[...]).astype(jnp.bfloat16).astype(jnp.float32)
    for turn in range(rows):
        grid[:, turn, :] = correlation[turn]
    cells = grid[...].reshape(kept * slots, lanes).astype(jnp.bfloat16)
    for pack in range(block // 16):
        shifted = jnp.dot(
            cells, moves[:, pack * 2 * lanes : (pack + 1) * 2 * lanes], preferred_element_type=jnp.float32
        )
        for j in range(kept):
            piece = shifted[j * slots : (j + 1) * slots]
            both = jnp.concatenate([piece[:, :lanes], piece[:, lanes:]], axis=0)
            start = (j + 1) * block + pack * 16
            taps[start : start + 16, :] = both.astype(jnp.bfloat16)

    def windows(ref, size, first_at):
        return jnp.concatenate(
            [ref[pl.ds(pl.multiple_of((first_at + n) * size, 16), 3 * size), :] for n in range(2)], axis=1
        )

    lead_one = half * (columns - reach_one - off)
    for t in range(0, reach_one, 2):
        product = jnp.dot(w1_ref[...], windows(taps, block, lead_one + t), preferred_element_type=jnp.float32)
        value = jnp.maximum(product, 0.0).astype(jnp.bfloat16)
        for n in range(2):
            first[(t + n + 1) * band : (t + n + 2) * band, :] = value[:, n * lanes : (n + 1) * lanes]

    lines, spots = masks(depth)
    for t in range(0, reach_two, 2):
        window = windows(first, band, 2 * half + t)
        for turn in range(rows):
            product = jnp.dot(
                w2_ref[turn * 9 * depth : (turn + 1) * 9 * depth, :], window, preferred_element_type=jnp.float32
            )
            for n in range(2):
                value = gathered(
                    lambda tap: product[tap * depth : (tap + 1) * depth, n * lanes : (n + 1) * lanes], lines, spots
                )
                start = (t + n + 1) * band + turn * depth
                second[start : start + depth, :] = value.astype(jnp.bfloat16)

    for t in range(0, share, 2):
        product = jnp.dot(w3_ref[...], windows(second, band, 2 * half + t), preferred_element_type=jnp.float32)
        for n in range(2):
            third[t + n] = product[:, n * lanes : (n + 1) * lanes]

    lines, spots = masks(share)
    peak = None
    for turn in range(rows):
        value = gathered(lambda tap: third[:, turn * 16 + tap, :], lines, spots)
        scores[turn, :share] = value
        top = jnp.max(value, axis=0, keepdims=True)
        peak = top if peak is None else jnp.maximum(peak, top)
    peak = jnp.broadcast_to(peak, (8, lanes))
    for turn in range(rows):
        scores[turn, share:] = peak

    def give(to):
        return pltpu.make_async_remote_copy(
            src_ref=scores.at[to], dst_ref=got_scores.at[row],
            send_sem=score_send.at[0], recv_sem=score_recv.at[0],
            device_id={"row": to}, device_id_type=MESH,
        )

    others = [(1 - team) * HALVES + n for n in range(HALVES)] + [row + 1 - 2 * half]
    for to in others:
        give(to).start()
    got_scores[row] = scores[row]

    sent(held.at[pl.ds(0, (groups - 1) * local_images)], hop_send.at[0])
    sent(picked.at[pl.ds(0, groups - 1)], pick_send.at[0])
    for pair in range(group_pairs):
        @pl.when(pair * HALVES + side != row)
        def _():
            sent(picked.at[0, 0], pick_send.at[0])

    arrived(got_scores.at[pl.ds(0, rows - 1)], score_recv.at[0])
    for pair in range(group_pairs):
        source_best = got_scores[pair * HALVES, share : share + 1, :]
        for part in range(1, HALVES):
            source_best = jnp.maximum(source_best, got_scores[pair * HALVES + part, share : share + 1, :])
        for part in range(HALVES):
            value = got_scores[pair * HALVES + part, :share]
            target_best = jnp.max(value, axis=-1, keepdims=True)
            o_ref[pair, 0, part * share : (part + 1) * share, :] = (
                value / (source_best + EPSILON) * (value / (target_best + EPSILON))
            ).astype(o_ref.dtype)

    sent(got_scores.at[pl.ds(0, rows - 1)], score_send.at[0])


def spread(features, src_ids, tgt_ids, image_slot, w_first, w_mid, w_last):
    groups = lax.axis_size("pair")
    rows = lax.axis_size("row")
    local_images, _, columns, channels = features.shape
    chunk = channels // groups
    depth = w_mid.shape[1]
    group_pairs = src_ids.shape[0] // groups
    positions = rows * columns
    band = rows * depth
    share = columns // HALVES
    kept = share + 8
    slots = 8
    block = 10 * slots
    vmem = pl.BlockSpec(memory_space=pltpu.VMEM)
    dma = pltpu.SemaphoreType.DMA
    bf16, f32 = jnp.bfloat16, jnp.float32
    weights = (w_first.transpose(2, 1, 0)[0], w_mid.transpose(1, 2, 0), w_last.transpose(1, 2, 0)[0])
    result = pl.pallas_call(
        spread_kernel,
        out_shape=pltpu.VMEM((group_pairs, 1, columns, positions), f32),
        in_specs=[pl.BlockSpec(memory_space=pltpu.HBM)] * 7,
        out_specs=vmem,
        scratch_shapes=[
            pltpu.VMEM(features.shape, bf16),
            *(pltpu.VMEM(weight.shape, bf16) for weight in weights),
            *(pltpu.SMEM(ids.shape, jnp.int32) for ids in (src_ids, tgt_ids, image_slot)),
            dma((7,)),
            pltpu.VMEM((band, 3 * block), bf16),
            pltpu.VMEM((9 * band, 3 * band), bf16),
            pltpu.VMEM((rows * 16, 3 * band), bf16),
            pltpu.VMEM((positions, 10 * positions), bf16),
            pltpu.VMEM((groups, local_images, columns, chunk), bf16),
            pltpu.VMEM((groups * local_images, columns, chunk), bf16),
            pltpu.VMEM((groups, group_pairs, 2, columns, chunk), bf16),
            pltpu.VMEM((groups // HALVES, rows, 2, columns, chunk), bf16),
            pltpu.VMEM((rows, columns, positions), f32),
            pltpu.VMEM((rows, kept, positions), f32),
            pltpu.VMEM((kept, slots, positions), f32),
            pltpu.VMEM(((kept + 2) * block, positions), bf16),
            pltpu.VMEM(((share + 6) * band, positions), bf16),
            pltpu.VMEM(((share + 4) * band, positions), bf16),
            pltpu.VMEM((share, rows * 16, positions), f32),
            pltpu.VMEM((rows, share + 8, positions), f32),
            pltpu.VMEM((rows, share + 8, positions), f32),
            dma((1,)), dma((1,)),
            dma((1,)), dma((groups // HALVES,)),
            dma((2,)),
            dma((1,)), dma((1,)),
        ],
        compiler_params=pltpu.CompilerParams(
            collective_id=0, has_side_effects=True, vmem_limit_bytes=VMEM_LIMIT
        ),
    )(*(pltpu.with_memory_space_constraint(x, pltpu.HBM) for x in (features, *weights, src_ids, tgt_ids, image_slot)))
    return result.astype(bf16)


def program(features, src_ids, tgt_ids, image_slot, w_first, w_mid, w_last):
    groups = lax.axis_size("pair")
    rows = lax.axis_size("row")
    _, local_rows, columns, channels = features.shape
    fits = (
        local_rows == 1
        and groups % HALVES == 0
        and rows * groups == HALVES * src_ids.shape[0]
        and channels % (groups * 128) == 0
        and rows * columns == 128
        and columns == 32
        and rows == 2 * HALVES
        and w_mid.shape[1] == 16
    )
    run = spread if fits else local
    return run(features, src_ids, tgt_ids, image_slot, w_first, w_mid, w_last)


def solution(mesh):
    placed = (P("pair", "row", None, None), P(), P(), P(), P(), P(), P())
    return jax.shard_map(
        program, mesh=mesh, in_specs=placed, out_specs=P("pair", "row", None, None), check_vma=False
    )
```

```python
import jax
import jax.numpy as jnp
from jax import lax
from jax.experimental import pallas as pl
from jax.experimental.pallas import tpu as pltpu
from jax.sharding import PartitionSpec as P

WID = 32
HALVES = 2
HEAD = 2
VMEM_LIMIT = 16 << 20
MESH = pl.DeviceIdType.MESH


EPSILON = 1e-05
NORM_EPS = 1e-06


def with_halo(cells, sides, width):
    for axis, dim in sides:
        count = lax.axis_size(axis)
        ends = count - 1
        head = lax.slice_in_dim(cells, 0, width, axis=dim)
        tail = lax.slice_in_dim(cells, cells.shape[dim] - width, cells.shape[dim], axis=dim)
        cells = jnp.concatenate(
            [
                lax.ppermute(tail, axis, [(i, (i + 1) % count) for i in range(ends)]),
                cells,
                lax.ppermute(head, axis, [((i + 1) % count, i) for i in range(ends)]),
            ],
            axis=dim,
        )
    return cells


def slot_lookup(image_ids, image_slot):
    matches = image_ids[..., None] == jnp.arange(image_slot.shape[0], dtype=jnp.int32)
    return jnp.sum(jnp.where(matches, image_slot, 0), axis=-1)


def consensus_layer(tensor, weight, col_masks, is_last):
    group_pairs = tensor.shape[0]
    channels_in = tensor.shape[1]
    positions = tensor.shape[4]
    channels_out = weight.shape[1]
    rimmed = with_halo(tensor, (("row", 2),), 1)
    padded = jnp.pad(rimmed, ((0, 0), (0, 0), (0, 0), (1, 1), (0, 0)))
    matrix = (
        weight.reshape(9, 9, channels_out, channels_in)
        .transpose(1, 2, 0, 3)
        .reshape(9 * channels_out, 9 * channels_in)
    )
    results = []
    for member in range(group_pairs):
        stacked = jnp.stack(
            [padded[member, :, a, b : b + WID, :] for a in range(3) for b in range(3)]
        )
        product = jnp.dot(
            matrix,
            stacked.reshape(9 * channels_in, WID * positions),
            preferred_element_type=jnp.float32,
        )
        product = product.reshape(9, channels_out, WID, positions)
        summed = jnp.zeros((channels_out, WID, positions), jnp.float32)
        for c in range(3):
            for d in range(3):
                offset = (c - 1) * WID + (d - 1)
                widened = jnp.pad(product[c * 3 + d], ((0, 0), (0, 0), (WID + 1, WID + 1)))
                shifted = widened[:, :, WID + 1 + offset : WID + 1 + offset + positions]
                summed = summed + shifted * col_masks[d]
        outputs = [jax.nn.relu(summed)]
        results.append(jnp.stack(outputs, axis=1))
    result = jnp.stack(results, axis=0)
    if is_last:
        return result
    return result.astype(jnp.bfloat16)


def local(features, src_ids, tgt_ids, image_slot, w_first, w_mid, w_last):
    local_images, local_rows, columns, channels = features.shape
    block_rows = local_rows * columns
    flattened = features.reshape(local_images, block_rows, channels).astype(jnp.float32)
    scale = lax.rsqrt(jnp.sum(flattened * flattened, axis=-1, keepdims=True) + NORM_EPS)
    normed = (flattened * scale).astype(jnp.bfloat16)
    group_pairs = src_ids.shape[0] // lax.axis_size("pair")
    pair_index = lax.axis_index("pair")
    wanted_ids = jnp.stack([src_ids, tgt_ids], axis=1)
    own_ids = lax.dynamic_slice_in_dim(
        wanted_ids, pair_index * group_pairs, group_pairs, 0
    ).reshape(-1)
    needed = slot_lookup(own_ids, image_slot)
    shard_piece = lax.all_gather(normed, "pair", axis=0, tiled=True)
    length = shard_piece.shape[0]
    one_hot = (needed[:, None] == jnp.arange(length, dtype=jnp.int32)).astype(jnp.bfloat16)
    chosen = jnp.einsum("wk,krc->wrc", one_hot, shard_piece, preferred_element_type=jnp.float32)
    routed = chosen.astype(jnp.bfloat16)
    routed = routed.reshape(group_pairs, 2, block_rows, channels)
    sources = routed[:, 0]
    targets = routed[:, 1]
    correlation = jnp.einsum(
        "prc,ptc->prt",
        sources,
        lax.all_gather(targets, "row", axis=1, tiled=True),
        preferred_element_type=jnp.float32,
    )
    positions = correlation.shape[2]
    tensor = correlation.astype(jnp.bfloat16).reshape(
        group_pairs, 1, local_rows, columns, positions
    )
    target_col = jnp.arange(positions, dtype=jnp.int32) % WID
    col_masks = [
        ((target_col + d - 1 >= 0) & (target_col + d - 1 < WID)).astype(jnp.float32)
        for d in range(3)
    ]
    hidden_one = consensus_layer(tensor, w_first, col_masks, False)
    hidden_two = consensus_layer(hidden_one, w_mid, col_masks, False)
    consensus = consensus_layer(hidden_two, w_last, col_masks, True)[:, 0]
    target_best = jnp.max(consensus, axis=-1, keepdims=True)
    local_best = jnp.max(consensus, axis=(1, 2))
    source_best = lax.pmax(local_best, "row")
    matches = (
        consensus
        / (source_best[:, None, None, :] + EPSILON)
        * (consensus / (target_best + EPSILON))
    )
    return matches.astype(jnp.bfloat16)


def spread_kernel(
    x_any, wf_any, wm_any, wl_any, src_any, tgt_any, slot_any, o_ref,
    x_ref, wf_ref, wm_ref, wl_ref, src_ref, tgt_ref, slot_ref, load_sem,
    w1_ref, w2_ref, w3_ref, moves,
    parts, held, picked, chosen, partial, other, grid, taps, first, second, third,
    scores, got_scores,
    hop_send, hop_recv, pick_send, pick_recv, mate_sem, score_send, score_recv,
):
    groups = lax.axis_size("pair")
    rows = lax.axis_size("row")
    me = lax.axis_index("pair")
    row = lax.axis_index("row")
    group_pairs = rows // HALVES
    team = lax.div(row, HALVES)
    half = lax.rem(row, HALVES)
    local_images, columns, chunk = parts.shape[1:]
    positions = rows * columns
    lanes = o_ref.shape[3]
    depth = wm_ref.shape[0]
    band = rows * depth
    slots = grid.shape[1]
    share = columns // HALVES
    kept = grid.shape[0]
    reach_one, reach_two = share + 2, share + 2

    loads = [
        pltpu.make_async_copy(source, target, load_sem.at[n])
        for n, (source, target) in enumerate(
            (
                (x_any, x_ref), (wf_any, wf_ref), (wm_any, wm_ref), (wl_any, wl_ref),
                (src_any, src_ref), (tgt_any, tgt_ref), (slot_any, slot_ref),
            )
        )
    ]
    loads[0].start()
    barrier = pltpu.get_barrier_semaphore()
    for step in range(1, groups):
        pl.semaphore_signal(
            barrier, inc=1, device_id={"pair": lax.rem(me + step, groups)}, device_id_type=MESH
        )
    for turn in range(1, rows):
        pl.semaphore_signal(
            barrier, inc=1, device_id={"row": lax.rem(row + turn, rows)}, device_id_type=MESH
        )

    low, high = me, groups - 1 - me
    near, gap = jnp.minimum(low, high), jnp.abs(high - low)

    def distant(step):
        single = jnp.where(high > low, groups - 1 - step, step)
        beyond = step - gap
        away = near - lax.div(beyond, 2)
        double = me + jnp.where(lax.rem(beyond, 2) == 0, away, -away)
        return jnp.where(step < gap, single, double)

    peers = [distant(step) for step in range(groups - 1)]
    routes = [jnp.where(k < me, k, k + 1) for k in range(groups - 1)]

    for load in loads[1:]:
        load.start()
    loads[0].wait()

    for image in range(local_images):
        cells = x_ref[image, 0].astype(jnp.float32)
        scale = lax.rsqrt(jnp.sum(cells * cells, axis=-1, keepdims=True) + NORM_EPS)
        normed = (cells * scale).astype(jnp.bfloat16)
        for piece in range(groups):
            parts[piece, image] = normed[:, piece * chunk : (piece + 1) * chunk]
    held[pl.ds(me * local_images, local_images)] = parts[me]
    pl.semaphore_wait(barrier, groups + rows - 2)

    def arrived(where, semaphore):
        pltpu.make_async_remote_copy(
            src_ref=where, dst_ref=where, send_sem=semaphore, recv_sem=semaphore,
            device_id={"row": row}, device_id_type=MESH,
        ).wait_recv()

    def sent(where, semaphore):
        pltpu.make_async_remote_copy(
            src_ref=where, dst_ref=where, send_sem=semaphore, recv_sem=semaphore,
            device_id={"row": row}, device_id_type=MESH,
        ).wait_send()

    def hop(peer, slot):
        return pltpu.make_async_remote_copy(
            src_ref=parts.at[peer],
            dst_ref=held.at[pl.ds(slot * local_images, local_images)],
            send_sem=hop_send.at[0], recv_sem=hop_recv.at[0],
            device_id={"pair": peer}, device_id_type=MESH,
        )

    for to in peers:
        hop(to, me).start()

    grid[...] = jnp.zeros_like(grid)
    block = taps.shape[0] // (kept + 2)
    for edge in (0, kept + 1):
        taps[edge * block : (edge + 1) * block, :] = jnp.zeros((block, lanes), taps.dtype)
    for edge in (0, reach_one + 1):
        first[edge * band : (edge + 1) * band, :] = jnp.zeros((band, lanes), first.dtype)
    for edge in (0, reach_two + 1):
        second[edge * band : (edge + 1) * band, :] = jnp.zeros((band, lanes), second.dtype)

    def select(shape, test):
        i = lax.broadcasted_iota(jnp.int32, shape, 0)
        m = lax.broadcasted_iota(jnp.int32, shape, 1)
        return test(i, m)

    for tap in range(10):
        c, d = tap // 3, tap % 3

        def reaches(i, m):
            line = lax.div(m, columns) + c - 1
            spot = lax.rem(m, columns) + d - 1
            return (i == line * columns + spot) & (line >= 0) & (line < rows) & (spot >= 0) & (spot < columns)

        if tap < 9:
            move = select((lanes, lanes), reaches).astype(jnp.bfloat16)
        else:
            move = jnp.zeros((lanes, lanes), jnp.bfloat16)
        moves[:, tap * lanes : (tap + 1) * lanes] = move

    for load in loads[1:]:
        load.wait()
    count = wf_ref.shape[1]
    kernels = jnp.concatenate([wm_ref[...].reshape(depth * depth, count), wl_ref[...]], axis=0)
    height = kernels.shape[0]
    wide = 2 * lanes
    matching = select((height, wide), lambda i, m: lax.rem(i, depth) == lax.rem(m, depth))
    folding = select((32, height), lambda i, m: lax.div(m, depth) == i).astype(jnp.bfloat16)
    line_of = select((32, wide), lambda i, m: lax.div(lax.rem(m, band), depth))
    last_rows = [[] for _ in range(rows)]
    for tap in range(9):
        here = select(
            (count, wide),
            lambda i, m: (i == (lax.div(lax.rem(m, band), depth) * 3 + lax.div(m, band)) * 9 + tap)
            & (lax.rem(m, band) < 3 * depth)
            & (m < 3 * band),
        ).astype(jnp.bfloat16)
        picks = jnp.dot(kernels, here, preferred_element_type=jnp.float32)
        picks = jnp.where(matching, picks, 0.0).astype(jnp.bfloat16)
        folded = jnp.dot(folding, picks, preferred_element_type=jnp.float32)
        for turn in range(rows):
            shift = ((turn - 1) * depth) % wide
            moved = pltpu.roll(folded, shift, 1) if shift else folded
            moved = jnp.where((line_of >= turn - 1) & (line_of <= turn + 1), moved, 0.0)[:, : 3 * band]
            start = (turn * 9 + tap) * depth
            w2_ref[start : start + depth, :] = moved[:depth].astype(jnp.bfloat16)
            last_rows[turn].append(moved[depth : depth + 1])
    for turn in range(rows):
        last = jnp.concatenate(last_rows[turn] + [jnp.zeros((16 - 9, 3 * band), jnp.float32)], axis=0)
        w3_ref[turn * 16 : (turn + 1) * 16, :] = last.astype(jnp.bfloat16)

    for turn in range(rows):
        def uses(i, m):
            inside = lax.rem(m, block)
            a = lax.rem(inside, rows) - turn + 1
            tap = lax.div(inside, rows)
            return (i == 27 * a + 9 * lax.div(m, block) + tap) & (a >= 0) & (a < 3) & (tap < 9)

        here = select((count, 3 * block), uses).astype(jnp.bfloat16)
        packed = jnp.dot(wf_ref[...], here, preferred_element_type=jnp.float32)
        w1_ref[turn * depth : (turn + 1) * depth, :] = packed.astype(jnp.bfloat16)

    def masks(size):
        place = lax.broadcasted_iota(jnp.int32, (size, lanes), 1)
        line = lax.div(place, columns)
        spot = lax.rem(place, columns)
        lines = [((line + c - 1 >= 0) & (line + c - 1 < rows)).astype(jnp.float32) for c in range(3)]
        spots = [((spot + d - 1 >= 0) & (spot + d - 1 < columns)).astype(jnp.float32) for d in range(3)]
        return lines, spots

    def gathered(term_at, lines, spots):
        summed = None
        for c in range(3):
            inner = None
            for d in range(3):
                term = term_at(c * 3 + d)
                if d != 1:
                    term = pltpu.roll(term, (1 - d) % lanes, 1) * spots[d]
                inner = term if inner is None else inner + term
            if c != 1:
                inner = pltpu.roll(inner, ((1 - c) * columns) % lanes, 1) * lines[c]
            summed = inner if summed is None else summed + inner
        return jnp.maximum(summed, 0.0)

    wanted = {}
    for step, to in enumerate(routes + [me]):
        for pair in range(group_pairs):
            index = to * group_pairs + pair
            wanted[step, pair] = slot_ref[src_ref[index]], slot_ref[tgt_ref[index]]
    arrived(held.at[pl.ds(0, (groups - 1) * local_images)], hop_recv.at[0])

    lot = lax.div(me, HALVES)
    side = lax.rem(me, HALVES)

    def pick(to, pair):
        return pltpu.make_async_remote_copy(
            src_ref=picked.at[to, pair], dst_ref=chosen.at[lot, row],
            send_sem=pick_send.at[0], recv_sem=pick_recv.at[lot],
            device_id={"pair": to, "row": pair * HALVES + side}, device_id_type=MESH,
        )

    def gather_pick(step, to, pair):
        source_slot, target_slot = wanted[step, pair]
        source_image = held[source_slot]
        target_image = held[target_slot]
        picked[to, pair, 0] = source_image
        picked[to, pair, 1] = target_image
        if to is me:
            @pl.when(pair * HALVES + side == row)
            def _():
                pltpu.make_async_copy(picked.at[me, pair], chosen.at[lot, row], pick_recv.at[lot]).start()

    def send_pick(to, pair):
        if to is not me:
            pick(to, pair).start()
        else:
            @pl.when(pair * HALVES + side != row)
            def _():
                pick(to, pair).start()

    turns = [(step, to, pair) for step, to in enumerate(routes + [me]) for pair in reversed(range(group_pairs))]
    for part in (turns[:HEAD], turns[HEAD:]):
        for step, to, pair in part:
            gather_pick(step, to, pair)
        for step, to, pair in part:
            send_pick(to, pair)

    total = jnp.zeros((positions, positions), jnp.float32)
    teams = groups // HALVES
    toward = jnp.where(lot < teams // 2, 1, -1)
    for step in range(teams):
        piece = lax.rem(lot + toward * step + teams, teams)
        arrived(chosen.at[piece], pick_recv.at[piece])
        left = jnp.concatenate([chosen[piece, turn, 0] for turn in range(rows)], axis=0)
        right = jnp.concatenate([chosen[piece, turn, 1] for turn in range(rows)], axis=0)
        total = total + lax.dot_general(
            left, right, (((1,), (1,)), ((), ())), preferred_element_type=jnp.float32
        )
    partial[...] = total.reshape(partial.shape)
    off = columns - kept
    swap = pltpu.make_async_remote_copy(
        src_ref=partial.at[:, pl.ds(pl.multiple_of((1 - half) * off, off), kept)],
        dst_ref=other, send_sem=mate_sem.at[0], recv_sem=mate_sem.at[1],
        device_id={"row": row + 1 - 2 * half}, device_id_type=MESH,
    )
    swap.start()
    swap.wait()
    mine = partial[:, pl.ds(pl.multiple_of(half * off, off), kept), :]
    correlation = (mine + other[...]).astype(jnp.bfloat16).astype(jnp.float32)
    for turn in range(rows):
        grid[:, turn, :] = correlation[turn]
        grid[:, rows + turn, :] = correlation[turn]
    cells = grid[...].reshape(kept * slots, lanes).astype(jnp.bfloat16)
    upper = lax.broadcasted_iota(jnp.int32, (slots, lanes), 0) < rows
    blank = jnp.zeros((slots, lanes), jnp.float32)
    for pack in range(block // 16):
        moved = moves[:, pack * 4 * lanes : min(pack * 4 + 4, 10) * lanes]
        shifted = jnp.dot(cells, moved, preferred_element_type=jnp.float32)
        for j in range(kept):
            piece = shifted[j * slots : (j + 1) * slots]
            pairs = [
                jnp.where(upper, piece[:, n * lanes : (n + 1) * lanes], piece[:, (n + 1) * lanes : (n + 2) * lanes])
                for n in range(0, moved.shape[1] // lanes, 2)
            ]
            both = jnp.concatenate((pairs + [blank])[:2], axis=0)
            start = (j + 1) * block + pack * 16
            taps[start : start + 16, :] = both.astype(jnp.bfloat16)

    def windows(ref, size, first_at):
        return jnp.concatenate(
            [ref[pl.ds(pl.multiple_of((first_at + n) * size, 16), 3 * size), :] for n in range(2)], axis=1
        )

    lead_one = half * (columns - reach_one - off)
    for t in range(0, reach_one, 2):
        product = jnp.dot(w1_ref[...], windows(taps, block, lead_one + t), preferred_element_type=jnp.float32)
        value = jnp.maximum(product, 0.0).astype(jnp.bfloat16)
        for n in range(2):
            first[(t + n + 1) * band : (t + n + 2) * band, :] = value[:, n * lanes : (n + 1) * lanes]

    lines, spots = masks(depth)
    for t in range(0, reach_two, 2):
        window = windows(first, band, (reach_one - reach_two) * half + t)
        for turn in range(rows):
            product = jnp.dot(
                w2_ref[turn * 9 * depth : (turn + 1) * 9 * depth, :], window, preferred_element_type=jnp.float32
            )
            for n in range(2):
                value = gathered(
                    lambda tap: product[tap * depth : (tap + 1) * depth, n * lanes : (n + 1) * lanes], lines, spots
                )
                start = (t + n + 1) * band + turn * depth
                second[start : start + depth, :] = value.astype(jnp.bfloat16)

    for t in range(0, share, 2):
        product = jnp.dot(w3_ref[...], windows(second, band, 2 * half + t), preferred_element_type=jnp.float32)
        for n in range(2):
            third[t + n] = product[:, n * lanes : (n + 1) * lanes]

    lines, spots = masks(share)
    peak = None
    for turn in range(rows):
        value = gathered(lambda tap: third[:, turn * 16 + tap, :], lines, spots)
        scores[turn, :share] = value
        top = jnp.max(value, axis=0, keepdims=True)
        peak = top if peak is None else jnp.maximum(peak, top)
    peak = jnp.broadcast_to(peak, (8, lanes))
    for turn in range(rows):
        scores[turn, share:] = peak

    def give(to):
        return pltpu.make_async_remote_copy(
            src_ref=scores.at[to], dst_ref=got_scores.at[row],
            send_sem=score_send.at[0], recv_sem=score_recv.at[0],
            device_id={"row": to}, device_id_type=MESH,
        )

    others = [(1 - team) * HALVES + n for n in range(HALVES)] + [row + 1 - 2 * half]
    for to in others:
        give(to).start()
    got_scores[row] = scores[row]

    sent(held.at[pl.ds(0, (groups - 1) * local_images)], hop_send.at[0])
    sent(picked.at[pl.ds(0, groups - 1)], pick_send.at[0])
    for pair in range(group_pairs):
        @pl.when(pair * HALVES + side != row)
        def _():
            sent(picked.at[0, 0], pick_send.at[0])

    arrived(got_scores.at[pl.ds(0, rows - 1)], score_recv.at[0])
    for pair in range(group_pairs):
        source_best = got_scores[pair * HALVES, share : share + 1, :]
        for part in range(1, HALVES):
            source_best = jnp.maximum(source_best, got_scores[pair * HALVES + part, share : share + 1, :])
        for part in range(HALVES):
            value = got_scores[pair * HALVES + part, :share]
            target_best = jnp.max(value, axis=-1, keepdims=True)
            o_ref[pair, 0, part * share : (part + 1) * share, :] = (
                value / (source_best + EPSILON) * (value / (target_best + EPSILON))
            ).astype(o_ref.dtype)

    sent(got_scores.at[pl.ds(0, rows - 1)], score_send.at[0])


def spread(features, src_ids, tgt_ids, image_slot, w_first, w_mid, w_last):
    groups = lax.axis_size("pair")
    rows = lax.axis_size("row")
    local_images, _, columns, channels = features.shape
    chunk = channels // groups
    depth = w_mid.shape[1]
    group_pairs = src_ids.shape[0] // groups
    positions = rows * columns
    band = rows * depth
    share = columns // HALVES
    kept = share + 8
    slots = 2 * rows
    block = 48
    vmem = pl.BlockSpec(memory_space=pltpu.VMEM)
    dma = pltpu.SemaphoreType.DMA
    bf16, f32 = jnp.bfloat16, jnp.float32
    weights = (w_first.transpose(2, 1, 0)[0], w_mid.transpose(1, 2, 0), w_last.transpose(1, 2, 0)[0])
    result = pl.pallas_call(
        spread_kernel,
        out_shape=pltpu.VMEM((group_pairs, 1, columns, positions), f32),
        in_specs=[pl.BlockSpec(memory_space=pltpu.HBM)] * 7,
        out_specs=vmem,
        scratch_shapes=[
            pltpu.VMEM(features.shape, bf16),
            *(pltpu.VMEM(weight.shape, bf16) for weight in weights),
            *(pltpu.SMEM(ids.shape, jnp.int32) for ids in (src_ids, tgt_ids, image_slot)),
            dma((7,)),
            pltpu.VMEM((band, 3 * block), bf16),
            pltpu.VMEM((9 * band, 3 * band), bf16),
            pltpu.VMEM((rows * 16, 3 * band), bf16),
            pltpu.VMEM((positions, 10 * positions), bf16),
            pltpu.VMEM((groups, local_images, columns, chunk), bf16),
            pltpu.VMEM((groups * local_images, columns, chunk), bf16),
            pltpu.VMEM((groups, group_pairs, 2, columns, chunk), bf16),
            pltpu.VMEM((groups // HALVES, rows, 2, columns, chunk), bf16),
            pltpu.VMEM((rows, columns, positions), f32),
            pltpu.VMEM((rows, kept, positions), f32),
            pltpu.VMEM((kept, slots, positions), f32),
            pltpu.VMEM(((kept + 2) * block, positions), bf16),
            pltpu.VMEM(((share + 4) * band, positions), bf16),
            pltpu.VMEM(((share + 4) * band, positions), bf16),
            pltpu.VMEM((share, rows * 16, positions), f32),
            pltpu.VMEM((rows, share + 8, positions), f32),
            pltpu.VMEM((rows, share + 8, positions), f32),
            dma((1,)), dma((1,)),
            dma((1,)), dma((groups // HALVES,)),
            dma((2,)),
            dma((1,)), dma((1,)),
        ],
        compiler_params=pltpu.CompilerParams(
            collective_id=0, has_side_effects=True, vmem_limit_bytes=VMEM_LIMIT
        ),
    )(*(pltpu.with_memory_space_constraint(x, pltpu.HBM) for x in (features, *weights, src_ids, tgt_ids, image_slot)))
    return result.astype(bf16)


def program(features, src_ids, tgt_ids, image_slot, w_first, w_mid, w_last):
    groups = lax.axis_size("pair")
    rows = lax.axis_size("row")
    _, local_rows, columns, channels = features.shape
    fits = (
        local_rows == 1
        and groups % HALVES == 0
        and rows * groups == HALVES * src_ids.shape[0]
        and channels % (groups * 128) == 0
        and rows * columns == 128
        and columns == 32
        and rows == 2 * HALVES
        and w_mid.shape[1] == 16
    )
    run = spread if fits else local
    return run(features, src_ids, tgt_ids, image_slot, w_first, w_mid, w_last)


def solution(mesh):
    placed = (P("pair", "row", None, None), P(), P(), P(), P(), P(), P())
    return jax.shard_map(
        program, mesh=mesh, in_specs=placed, out_specs=P("pair", "row", None, None), check_vma=False
    )
```

```python
import jax
import jax.numpy as jnp
from jax import lax
from jax.experimental import pallas as pl
from jax.experimental.pallas import tpu as pltpu
from jax.sharding import PartitionSpec as P

WID = 32
HALVES = 2
HEAD = 1
VMEM_LIMIT = 16 << 20
MESH = pl.DeviceIdType.MESH


EPSILON = 1e-05
NORM_EPS = 1e-06


def with_halo(cells, sides, width):
    for axis, dim in sides:
        count = lax.axis_size(axis)
        ends = count - 1
        head = lax.slice_in_dim(cells, 0, width, axis=dim)
        tail = lax.slice_in_dim(cells, cells.shape[dim] - width, cells.shape[dim], axis=dim)
        cells = jnp.concatenate(
            [
                lax.ppermute(tail, axis, [(i, (i + 1) % count) for i in range(ends)]),
                cells,
                lax.ppermute(head, axis, [((i + 1) % count, i) for i in range(ends)]),
            ],
            axis=dim,
        )
    return cells


def slot_lookup(image_ids, image_slot):
    matches = image_ids[..., None] == jnp.arange(image_slot.shape[0], dtype=jnp.int32)
    return jnp.sum(jnp.where(matches, image_slot, 0), axis=-1)


def consensus_layer(tensor, weight, col_masks, is_last):
    group_pairs = tensor.shape[0]
    channels_in = tensor.shape[1]
    positions = tensor.shape[4]
    channels_out = weight.shape[1]
    rimmed = with_halo(tensor, (("row", 2),), 1)
    padded = jnp.pad(rimmed, ((0, 0), (0, 0), (0, 0), (1, 1), (0, 0)))
    matrix = (
        weight.reshape(9, 9, channels_out, channels_in)
        .transpose(1, 2, 0, 3)
        .reshape(9 * channels_out, 9 * channels_in)
    )
    results = []
    for member in range(group_pairs):
        stacked = jnp.stack(
            [padded[member, :, a, b : b + WID, :] for a in range(3) for b in range(3)]
        )
        product = jnp.dot(
            matrix,
            stacked.reshape(9 * channels_in, WID * positions),
            preferred_element_type=jnp.float32,
        )
        product = product.reshape(9, channels_out, WID, positions)
        summed = jnp.zeros((channels_out, WID, positions), jnp.float32)
        for c in range(3):
            for d in range(3):
                offset = (c - 1) * WID + (d - 1)
                widened = jnp.pad(product[c * 3 + d], ((0, 0), (0, 0), (WID + 1, WID + 1)))
                shifted = widened[:, :, WID + 1 + offset : WID + 1 + offset + positions]
                summed = summed + shifted * col_masks[d]
        outputs = [jax.nn.relu(summed)]
        results.append(jnp.stack(outputs, axis=1))
    result = jnp.stack(results, axis=0)
    if is_last:
        return result
    return result.astype(jnp.bfloat16)


def local(features, src_ids, tgt_ids, image_slot, w_first, w_mid, w_last):
    local_images, local_rows, columns, channels = features.shape
    block_rows = local_rows * columns
    flattened = features.reshape(local_images, block_rows, channels).astype(jnp.float32)
    scale = lax.rsqrt(jnp.sum(flattened * flattened, axis=-1, keepdims=True) + NORM_EPS)
    normed = (flattened * scale).astype(jnp.bfloat16)
    group_pairs = src_ids.shape[0] // lax.axis_size("pair")
    pair_index = lax.axis_index("pair")
    wanted_ids = jnp.stack([src_ids, tgt_ids], axis=1)
    own_ids = lax.dynamic_slice_in_dim(
        wanted_ids, pair_index * group_pairs, group_pairs, 0
    ).reshape(-1)
    needed = slot_lookup(own_ids, image_slot)
    shard_piece = lax.all_gather(normed, "pair", axis=0, tiled=True)
    length = shard_piece.shape[0]
    one_hot = (needed[:, None] == jnp.arange(length, dtype=jnp.int32)).astype(jnp.bfloat16)
    chosen = jnp.einsum("wk,krc->wrc", one_hot, shard_piece, preferred_element_type=jnp.float32)
    routed = chosen.astype(jnp.bfloat16)
    routed = routed.reshape(group_pairs, 2, block_rows, channels)
    sources = routed[:, 0]
    targets = routed[:, 1]
    correlation = jnp.einsum(
        "prc,ptc->prt",
        sources,
        lax.all_gather(targets, "row", axis=1, tiled=True),
        preferred_element_type=jnp.float32,
    )
    positions = correlation.shape[2]
    tensor = correlation.astype(jnp.bfloat16).reshape(
        group_pairs, 1, local_rows, columns, positions
    )
    target_col = jnp.arange(positions, dtype=jnp.int32) % WID
    col_masks = [
        ((target_col + d - 1 >= 0) & (target_col + d - 1 < WID)).astype(jnp.float32)
        for d in range(3)
    ]
    hidden_one = consensus_layer(tensor, w_first, col_masks, False)
    hidden_two = consensus_layer(hidden_one, w_mid, col_masks, False)
    consensus = consensus_layer(hidden_two, w_last, col_masks, True)[:, 0]
    target_best = jnp.max(consensus, axis=-1, keepdims=True)
    local_best = jnp.max(consensus, axis=(1, 2))
    source_best = lax.pmax(local_best, "row")
    matches = (
        consensus
        / (source_best[:, None, None, :] + EPSILON)
        * (consensus / (target_best + EPSILON))
    )
    return matches.astype(jnp.bfloat16)


def spread_kernel(
    x_any, wf_any, wm_any, wl_any, src_any, tgt_any, slot_any, o_ref,
    x_ref, wf_ref, wm_ref, wl_ref, src_ref, tgt_ref, slot_ref, load_sem,
    w1_ref, w2_ref, w3_ref, moves,
    parts, held, picked, chosen, partial, other, grid, taps, first, second, third,
    scores, got_scores,
    hop_send, hop_recv, pick_send, pick_recv, mate_sem, score_send, score_recv,
):
    groups = lax.axis_size("pair")
    rows = lax.axis_size("row")
    me = lax.axis_index("pair")
    row = lax.axis_index("row")
    group_pairs = rows // HALVES
    team = lax.div(row, HALVES)
    half = lax.rem(row, HALVES)
    local_images, columns, chunk = parts.shape[1:]
    positions = rows * columns
    lanes = o_ref.shape[3]
    depth = wm_ref.shape[0]
    band = rows * depth
    slots = grid.shape[1]
    share = columns // HALVES
    kept = grid.shape[0]
    reach_one, reach_two = share + 2, share + 2

    loads = [
        pltpu.make_async_copy(source, target, load_sem.at[n])
        for n, (source, target) in enumerate(
            (
                (x_any, x_ref), (wf_any, wf_ref), (wm_any, wm_ref), (wl_any, wl_ref),
                (src_any, src_ref), (tgt_any, tgt_ref), (slot_any, slot_ref),
            )
        )
    ]
    loads[0].start()
    barrier = pltpu.get_barrier_semaphore()
    for step in range(1, groups):
        pl.semaphore_signal(
            barrier, inc=1, device_id={"pair": lax.rem(me + step, groups)}, device_id_type=MESH
        )
    for turn in range(1, rows):
        pl.semaphore_signal(
            barrier, inc=1, device_id={"row": lax.rem(row + turn, rows)}, device_id_type=MESH
        )

    low, high = me, groups - 1 - me
    near, gap = jnp.minimum(low, high), jnp.abs(high - low)

    def distant(step):
        single = jnp.where(high > low, groups - 1 - step, step)
        beyond = step - gap
        away = near - lax.div(beyond, 2)
        double = me + jnp.where(lax.rem(beyond, 2) == 0, away, -away)
        return jnp.where(step < gap, single, double)

    peers = [distant(step) for step in range(groups - 1)]
    routes = [jnp.where(k < me, k, k + 1) for k in range(groups - 1)]

    for load in loads[1:]:
        load.start()
    loads[0].wait()

    for image in range(local_images):
        cells = x_ref[image, 0].astype(jnp.float32)
        scale = lax.rsqrt(jnp.sum(cells * cells, axis=-1, keepdims=True) + NORM_EPS)
        normed = (cells * scale).astype(jnp.bfloat16)
        for piece in range(groups):
            parts[piece, image] = normed[:, piece * chunk : (piece + 1) * chunk]
    held[pl.ds(me * local_images, local_images)] = parts[me]
    pl.semaphore_wait(barrier, groups + rows - 2)

    def arrived(where, semaphore):
        pltpu.make_async_remote_copy(
            src_ref=where, dst_ref=where, send_sem=semaphore, recv_sem=semaphore,
            device_id={"row": row}, device_id_type=MESH,
        ).wait_recv()

    def sent(where, semaphore):
        pltpu.make_async_remote_copy(
            src_ref=where, dst_ref=where, send_sem=semaphore, recv_sem=semaphore,
            device_id={"row": row}, device_id_type=MESH,
        ).wait_send()

    def hop(peer, slot):
        return pltpu.make_async_remote_copy(
            src_ref=parts.at[peer],
            dst_ref=held.at[pl.ds(slot * local_images, local_images)],
            send_sem=hop_send.at[0], recv_sem=hop_recv.at[0],
            device_id={"pair": peer}, device_id_type=MESH,
        )

    for to in peers:
        hop(to, me).start()

    grid[...] = jnp.zeros_like(grid)
    block = taps.shape[0] // (kept + 2)
    for edge in (0, kept + 1):
        taps[edge * block : (edge + 1) * block, :] = jnp.zeros((block, lanes), taps.dtype)
    for edge in (0, reach_one + 1):
        first[edge * band : (edge + 1) * band, :] = jnp.zeros((band, lanes), first.dtype)
    for edge in (0, reach_two + 1):
        second[edge * band : (edge + 1) * band, :] = jnp.zeros((band, lanes), second.dtype)

    def select(shape, test):
        i = lax.broadcasted_iota(jnp.int32, shape, 0)
        m = lax.broadcasted_iota(jnp.int32, shape, 1)
        return test(i, m)

    for tap in range(10):
        c, d = tap // 3, tap % 3

        def reaches(i, m):
            line = lax.div(m, columns) + c - 1
            spot = lax.rem(m, columns) + d - 1
            return (i == line * columns + spot) & (line >= 0) & (line < rows) & (spot >= 0) & (spot < columns)

        if tap < 9:
            move = select((lanes, lanes), reaches).astype(jnp.bfloat16)
        else:
            move = jnp.zeros((lanes, lanes), jnp.bfloat16)
        moves[:, tap * lanes : (tap + 1) * lanes] = move

    for load in loads[1:]:
        load.wait()
    count = wf_ref.shape[1]
    kernels = jnp.concatenate([wm_ref[...].reshape(depth * depth, count), wl_ref[...]], axis=0)
    height = kernels.shape[0]
    wide = 2 * lanes
    matching = select((height, wide), lambda i, m: lax.rem(i, depth) == lax.rem(m, depth))
    folding = select((32, height), lambda i, m: lax.div(m, depth) == i).astype(jnp.bfloat16)
    line_of = select((32, wide), lambda i, m: lax.div(lax.rem(m, band), depth))
    last_rows = [[] for _ in range(rows)]
    for tap in range(9):
        here = select(
            (count, wide),
            lambda i, m: (i == (lax.div(lax.rem(m, band), depth) * 3 + lax.div(m, band)) * 9 + tap)
            & (lax.rem(m, band) < 3 * depth)
            & (m < 3 * band),
        ).astype(jnp.bfloat16)
        picks = jnp.dot(kernels, here, preferred_element_type=jnp.float32)
        picks = jnp.where(matching, picks, 0.0).astype(jnp.bfloat16)
        folded = jnp.dot(folding, picks, preferred_element_type=jnp.float32)
        for turn in range(rows):
            shift = ((turn - 1) * depth) % wide
            moved = pltpu.roll(folded, shift, 1) if shift else folded
            moved = jnp.where((line_of >= turn - 1) & (line_of <= turn + 1), moved, 0.0)[:, : 3 * band]
            start = (turn * 9 + tap) * depth
            w2_ref[start : start + depth, :] = moved[:depth].astype(jnp.bfloat16)
            last_rows[turn].append(moved[depth : depth + 1])
    for turn in range(rows):
        last = jnp.concatenate(last_rows[turn] + [jnp.zeros((16 - 9, 3 * band), jnp.float32)], axis=0)
        w3_ref[turn * 16 : (turn + 1) * 16, :] = last.astype(jnp.bfloat16)

    for turn in range(rows):
        def uses(i, m):
            inside = lax.rem(m, block)
            a = lax.rem(inside, rows) - turn + 1
            tap = lax.div(inside, rows)
            return (i == 27 * a + 9 * lax.div(m, block) + tap) & (a >= 0) & (a < 3) & (tap < 9)

        here = select((count, 3 * block), uses).astype(jnp.bfloat16)
        packed = jnp.dot(wf_ref[...], here, preferred_element_type=jnp.float32)
        w1_ref[turn * depth : (turn + 1) * depth, :] = packed.astype(jnp.bfloat16)

    def masks(size):
        place = lax.broadcasted_iota(jnp.int32, (size, lanes), 1)
        line = lax.div(place, columns)
        spot = lax.rem(place, columns)
        lines = [((line + c - 1 >= 0) & (line + c - 1 < rows)).astype(jnp.float32) for c in range(3)]
        spots = [((spot + d - 1 >= 0) & (spot + d - 1 < columns)).astype(jnp.float32) for d in range(3)]
        return lines, spots

    def gathered(term_at, lines, spots):
        summed = None
        for c in range(3):
            inner = None
            for d in range(3):
                term = term_at(c * 3 + d)
                if d != 1:
                    term = pltpu.roll(term, (1 - d) % lanes, 1) * spots[d]
                inner = term if inner is None else inner + term
            if c != 1:
                inner = pltpu.roll(inner, ((1 - c) * columns) % lanes, 1) * lines[c]
            summed = inner if summed is None else summed + inner
        return jnp.maximum(summed, 0.0)

    wanted = {}
    for step, to in enumerate(routes + [me]):
        for pair in range(group_pairs):
            index = to * group_pairs + pair
            wanted[step, pair] = slot_ref[src_ref[index]], slot_ref[tgt_ref[index]]
    arrived(held.at[pl.ds(0, (groups - 1) * local_images)], hop_recv.at[0])

    lot = lax.div(me, HALVES)
    side = lax.rem(me, HALVES)

    def pick(to, pair):
        return pltpu.make_async_remote_copy(
            src_ref=picked.at[to, pair], dst_ref=chosen.at[lot, row],
            send_sem=pick_send.at[0], recv_sem=pick_recv.at[lot],
            device_id={"pair": to, "row": pair * HALVES + side}, device_id_type=MESH,
        )

    def gather_pick(step, to, pair):
        source_slot, target_slot = wanted[step, pair]
        source_image = held[source_slot]
        target_image = held[target_slot]
        picked[to, pair, 0] = source_image
        picked[to, pair, 1] = target_image
        if to is me:
            @pl.when(pair * HALVES + side == row)
            def _():
                pltpu.make_async_copy(picked.at[me, pair], chosen.at[lot, row], pick_recv.at[lot]).start()

    def send_pick(to, pair):
        if to is not me:
            pick(to, pair).start()
        else:
            @pl.when(pair * HALVES + side != row)
            def _():
                pick(to, pair).start()

    turns = [(step, to, pair) for step, to in enumerate(routes + [me]) for pair in reversed(range(group_pairs))]
    for part in (turns[:HEAD], turns[HEAD:]):
        for step, to, pair in part:
            gather_pick(step, to, pair)
        for step, to, pair in part:
            send_pick(to, pair)

    total = jnp.zeros((positions, positions), jnp.float32)
    teams = groups // HALVES
    toward = jnp.where(lot < teams // 2, 1, -1)
    for step in range(teams):
        piece = lax.rem(lot + toward * step + teams, teams)
        arrived(chosen.at[piece], pick_recv.at[piece])
        left = jnp.concatenate([chosen[piece, turn, 0] for turn in range(rows)], axis=0)
        right = jnp.concatenate([chosen[piece, turn, 1] for turn in range(rows)], axis=0)
        total = total + lax.dot_general(
            left, right, (((1,), (1,)), ((), ())), preferred_element_type=jnp.float32
        )
    partial[...] = total.reshape(partial.shape)
    off = columns - kept
    swap = pltpu.make_async_remote_copy(
        src_ref=partial.at[:, pl.ds(pl.multiple_of((1 - half) * off, off), kept)],
        dst_ref=other, send_sem=mate_sem.at[0], recv_sem=mate_sem.at[1],
        device_id={"row": row + 1 - 2 * half}, device_id_type=MESH,
    )
    swap.start()
    swap.wait()
    mine = partial[:, pl.ds(pl.multiple_of(half * off, off), kept), :]
    correlation = (mine + other[...]).astype(jnp.bfloat16).astype(jnp.float32)
    for turn in range(rows):
        grid[:, turn, :] = correlation[turn]
        grid[:, rows + turn, :] = correlation[turn]
    cells = grid[...].reshape(kept * slots, lanes).astype(jnp.bfloat16)
    upper = lax.broadcasted_iota(jnp.int32, (slots, lanes), 0) < rows
    blank = jnp.zeros((slots, lanes), jnp.float32)
    for pack in range(block // 16):
        moved = moves[:, pack * 4 * lanes : min(pack * 4 + 4, 10) * lanes]
        shifted = jnp.dot(cells, moved, preferred_element_type=jnp.float32)
        for j in range(kept):
            piece = shifted[j * slots : (j + 1) * slots]
            pairs = [
                jnp.where(upper, piece[:, n * lanes : (n + 1) * lanes], piece[:, (n + 1) * lanes : (n + 2) * lanes])
                for n in range(0, moved.shape[1] // lanes, 2)
            ]
            both = jnp.concatenate((pairs + [blank])[:2], axis=0)
            start = (j + 1) * block + pack * 16
            taps[start : start + 16, :] = both.astype(jnp.bfloat16)

    def windows(ref, size, first_at):
        return jnp.concatenate(
            [ref[pl.ds(pl.multiple_of((first_at + n) * size, 16), 3 * size), :] for n in range(2)], axis=1
        )

    lead_one = half * (columns - reach_one - off)
    for t in range(0, reach_one, 2):
        product = jnp.dot(w1_ref[...], windows(taps, block, lead_one + t), preferred_element_type=jnp.float32)
        value = jnp.maximum(product, 0.0).astype(jnp.bfloat16)
        for n in range(2):
            first[(t + n + 1) * band : (t + n + 2) * band, :] = value[:, n * lanes : (n + 1) * lanes]

    lines, spots = masks(depth)
    for t in range(0, reach_two, 2):
        window = windows(first, band, (reach_one - reach_two) * half + t)
        for turn in range(rows):
            product = jnp.dot(
                w2_ref[turn * 9 * depth : (turn + 1) * 9 * depth, :], window, preferred_element_type=jnp.float32
            )
            for n in range(2):
                value = gathered(
                    lambda tap: product[tap * depth : (tap + 1) * depth, n * lanes : (n + 1) * lanes], lines, spots
                )
                start = (t + n + 1) * band + turn * depth
                second[start : start + depth, :] = value.astype(jnp.bfloat16)

    for t in range(0, share, 2):
        product = jnp.dot(w3_ref[...], windows(second, band, 2 * half + t), preferred_element_type=jnp.float32)
        for n in range(2):
            third[t + n] = product[:, n * lanes : (n + 1) * lanes]

    lines, spots = masks(share)
    peak = None
    for turn in range(rows):
        value = gathered(lambda tap: third[:, turn * 16 + tap, :], lines, spots)
        scores[turn, :share] = value
        top = jnp.max(value, axis=0, keepdims=True)
        peak = top if peak is None else jnp.maximum(peak, top)
    peak = jnp.broadcast_to(peak, (8, lanes))
    for turn in range(rows):
        scores[turn, share:] = peak

    def give(to):
        return pltpu.make_async_remote_copy(
            src_ref=scores.at[to], dst_ref=got_scores.at[row],
            send_sem=score_send.at[0], recv_sem=score_recv.at[0],
            device_id={"row": to}, device_id_type=MESH,
        )

    others = [(1 - team) * HALVES + n for n in range(HALVES)] + [row + 1 - 2 * half]
    for to in others:
        give(to).start()
    got_scores[row] = scores[row]

    sent(held.at[pl.ds(0, (groups - 1) * local_images)], hop_send.at[0])
    sent(picked.at[pl.ds(0, groups - 1)], pick_send.at[0])
    for pair in range(group_pairs):
        @pl.when(pair * HALVES + side != row)
        def _():
            sent(picked.at[0, 0], pick_send.at[0])

    arrived(got_scores.at[pl.ds(0, rows - 1)], score_recv.at[0])
    for pair in range(group_pairs):
        source_best = got_scores[pair * HALVES, share : share + 1, :]
        for part in range(1, HALVES):
            source_best = jnp.maximum(source_best, got_scores[pair * HALVES + part, share : share + 1, :])
        for part in range(HALVES):
            value = got_scores[pair * HALVES + part, :share]
            target_best = jnp.max(value, axis=-1, keepdims=True)
            o_ref[pair, 0, part * share : (part + 1) * share, :] = (
                value / (source_best + EPSILON) * (value / (target_best + EPSILON))
            ).astype(o_ref.dtype)

    sent(got_scores.at[pl.ds(0, rows - 1)], score_send.at[0])


def spread(features, src_ids, tgt_ids, image_slot, w_first, w_mid, w_last):
    groups = lax.axis_size("pair")
    rows = lax.axis_size("row")
    local_images, _, columns, channels = features.shape
    chunk = channels // groups
    depth = w_mid.shape[1]
    group_pairs = src_ids.shape[0] // groups
    positions = rows * columns
    band = rows * depth
    share = columns // HALVES
    kept = share + 8
    slots = 2 * rows
    block = 48
    vmem = pl.BlockSpec(memory_space=pltpu.VMEM)
    dma = pltpu.SemaphoreType.DMA
    bf16, f32 = jnp.bfloat16, jnp.float32
    weights = (w_first.transpose(2, 1, 0)[0], w_mid.transpose(1, 2, 0), w_last.transpose(1, 2, 0)[0])
    result = pl.pallas_call(
        spread_kernel,
        out_shape=pltpu.VMEM((group_pairs, 1, columns, positions), f32),
        in_specs=[pl.BlockSpec(memory_space=pltpu.HBM)] * 7,
        out_specs=vmem,
        scratch_shapes=[
            pltpu.VMEM(features.shape, bf16),
            *(pltpu.VMEM(weight.shape, bf16) for weight in weights),
            *(pltpu.SMEM(ids.shape, jnp.int32) for ids in (src_ids, tgt_ids, image_slot)),
            dma((7,)),
            pltpu.VMEM((band, 3 * block), bf16),
            pltpu.VMEM((9 * band, 3 * band), bf16),
            pltpu.VMEM((rows * 16, 3 * band), bf16),
            pltpu.VMEM((positions, 10 * positions), bf16),
            pltpu.VMEM((groups, local_images, columns, chunk), bf16),
            pltpu.VMEM((groups * local_images, columns, chunk), bf16),
            pltpu.VMEM((groups, group_pairs, 2, columns, chunk), bf16),
            pltpu.VMEM((groups // HALVES, rows, 2, columns, chunk), bf16),
            pltpu.VMEM((rows, columns, positions), f32),
            pltpu.VMEM((rows, kept, positions), f32),
            pltpu.VMEM((kept, slots, positions), f32),
            pltpu.VMEM(((kept + 2) * block, positions), bf16),
            pltpu.VMEM(((share + 4) * band, positions), bf16),
            pltpu.VMEM(((share + 4) * band, positions), bf16),
            pltpu.VMEM((share, rows * 16, positions), f32),
            pltpu.VMEM((rows, share + 8, positions), f32),
            pltpu.VMEM((rows, share + 8, positions), f32),
            dma((1,)), dma((1,)),
            dma((1,)), dma((groups // HALVES,)),
            dma((2,)),
            dma((1,)), dma((1,)),
        ],
        compiler_params=pltpu.CompilerParams(
            collective_id=0, has_side_effects=True, vmem_limit_bytes=VMEM_LIMIT
        ),
    )(*(pltpu.with_memory_space_constraint(x, pltpu.HBM) for x in (features, *weights, src_ids, tgt_ids, image_slot)))
    return result.astype(bf16)


def program(features, src_ids, tgt_ids, image_slot, w_first, w_mid, w_last):
    groups = lax.axis_size("pair")
    rows = lax.axis_size("row")
    _, local_rows, columns, channels = features.shape
    fits = (
        local_rows == 1
        and groups % HALVES == 0
        and rows * groups == HALVES * src_ids.shape[0]
        and channels % (groups * 128) == 0
        and rows * columns == 128
        and columns == 32
        and rows == 2 * HALVES
        and w_mid.shape[1] == 16
    )
    run = spread if fits else local
    return run(features, src_ids, tgt_ids, image_slot, w_first, w_mid, w_last)


def solution(mesh):
    placed = (P("pair", "row", None, None), P(), P(), P(), P(), P(), P())
    return jax.shard_map(
        program, mesh=mesh, in_specs=placed, out_specs=P("pair", "row", None, None), check_vma=False
    )
```

```python
import jax
import jax.numpy as jnp
from jax import lax
from jax.experimental import pallas as pl
from jax.experimental.pallas import tpu as pltpu
from jax.sharding import PartitionSpec as P

WID = 32
HALVES = 2
HEAD = 1
VMEM_LIMIT = 16 << 20
MESH = pl.DeviceIdType.MESH


EPSILON = 1e-05
NORM_EPS = 1e-06


def with_halo(cells, sides, width):
    for axis, dim in sides:
        count = lax.axis_size(axis)
        ends = count - 1
        head = lax.slice_in_dim(cells, 0, width, axis=dim)
        tail = lax.slice_in_dim(cells, cells.shape[dim] - width, cells.shape[dim], axis=dim)
        cells = jnp.concatenate(
            [
                lax.ppermute(tail, axis, [(i, (i + 1) % count) for i in range(ends)]),
                cells,
                lax.ppermute(head, axis, [((i + 1) % count, i) for i in range(ends)]),
            ],
            axis=dim,
        )
    return cells


def slot_lookup(image_ids, image_slot):
    matches = image_ids[..., None] == jnp.arange(image_slot.shape[0], dtype=jnp.int32)
    return jnp.sum(jnp.where(matches, image_slot, 0), axis=-1)


def consensus_layer(tensor, weight, col_masks, is_last):
    group_pairs = tensor.shape[0]
    channels_in = tensor.shape[1]
    positions = tensor.shape[4]
    channels_out = weight.shape[1]
    rimmed = with_halo(tensor, (("row", 2),), 1)
    padded = jnp.pad(rimmed, ((0, 0), (0, 0), (0, 0), (1, 1), (0, 0)))
    matrix = (
        weight.reshape(9, 9, channels_out, channels_in)
        .transpose(1, 2, 0, 3)
        .reshape(9 * channels_out, 9 * channels_in)
    )
    results = []
    for member in range(group_pairs):
        stacked = jnp.stack(
            [padded[member, :, a, b : b + WID, :] for a in range(3) for b in range(3)]
        )
        product = jnp.dot(
            matrix,
            stacked.reshape(9 * channels_in, WID * positions),
            preferred_element_type=jnp.float32,
        )
        product = product.reshape(9, channels_out, WID, positions)
        summed = jnp.zeros((channels_out, WID, positions), jnp.float32)
        for c in range(3):
            for d in range(3):
                offset = (c - 1) * WID + (d - 1)
                widened = jnp.pad(product[c * 3 + d], ((0, 0), (0, 0), (WID + 1, WID + 1)))
                shifted = widened[:, :, WID + 1 + offset : WID + 1 + offset + positions]
                summed = summed + shifted * col_masks[d]
        outputs = [jax.nn.relu(summed)]
        results.append(jnp.stack(outputs, axis=1))
    result = jnp.stack(results, axis=0)
    if is_last:
        return result
    return result.astype(jnp.bfloat16)


def local(features, src_ids, tgt_ids, image_slot, w_first, w_mid, w_last):
    local_images, local_rows, columns, channels = features.shape
    block_rows = local_rows * columns
    flattened = features.reshape(local_images, block_rows, channels).astype(jnp.float32)
    scale = lax.rsqrt(jnp.sum(flattened * flattened, axis=-1, keepdims=True) + NORM_EPS)
    normed = (flattened * scale).astype(jnp.bfloat16)
    group_pairs = src_ids.shape[0] // lax.axis_size("pair")
    pair_index = lax.axis_index("pair")
    wanted_ids = jnp.stack([src_ids, tgt_ids], axis=1)
    own_ids = lax.dynamic_slice_in_dim(
        wanted_ids, pair_index * group_pairs, group_pairs, 0
    ).reshape(-1)
    needed = slot_lookup(own_ids, image_slot)
    shard_piece = lax.all_gather(normed, "pair", axis=0, tiled=True)
    length = shard_piece.shape[0]
    one_hot = (needed[:, None] == jnp.arange(length, dtype=jnp.int32)).astype(jnp.bfloat16)
    chosen = jnp.einsum("wk,krc->wrc", one_hot, shard_piece, preferred_element_type=jnp.float32)
    routed = chosen.astype(jnp.bfloat16)
    routed = routed.reshape(group_pairs, 2, block_rows, channels)
    sources = routed[:, 0]
    targets = routed[:, 1]
    correlation = jnp.einsum(
        "prc,ptc->prt",
        sources,
        lax.all_gather(targets, "row", axis=1, tiled=True),
        preferred_element_type=jnp.float32,
    )
    positions = correlation.shape[2]
    tensor = correlation.astype(jnp.bfloat16).reshape(
        group_pairs, 1, local_rows, columns, positions
    )
    target_col = jnp.arange(positions, dtype=jnp.int32) % WID
    col_masks = [
        ((target_col + d - 1 >= 0) & (target_col + d - 1 < WID)).astype(jnp.float32)
        for d in range(3)
    ]
    hidden_one = consensus_layer(tensor, w_first, col_masks, False)
    hidden_two = consensus_layer(hidden_one, w_mid, col_masks, False)
    consensus = consensus_layer(hidden_two, w_last, col_masks, True)[:, 0]
    target_best = jnp.max(consensus, axis=-1, keepdims=True)
    local_best = jnp.max(consensus, axis=(1, 2))
    source_best = lax.pmax(local_best, "row")
    matches = (
        consensus
        / (source_best[:, None, None, :] + EPSILON)
        * (consensus / (target_best + EPSILON))
    )
    return matches.astype(jnp.bfloat16)


def spread_kernel(
    x_any, wf_any, wm_any, wl_any, src_any, tgt_any, slot_any, o_ref,
    x_ref, wf_ref, wm_ref, wl_ref, src_ref, tgt_ref, slot_ref, load_sem,
    w1_ref, w2_ref, w3_ref, moves,
    parts, held, picked, chosen, partial, other, grid, taps, first, second, third,
    scores, got_scores,
    hop_send, hop_recv, pick_send, pick_recv, mate_sem, score_send, score_recv,
):
    groups = lax.axis_size("pair")
    rows = lax.axis_size("row")
    me = lax.axis_index("pair")
    row = lax.axis_index("row")
    group_pairs = rows // HALVES
    team = lax.div(row, HALVES)
    half = lax.rem(row, HALVES)
    local_images, columns, chunk = parts.shape[1:]
    positions = rows * columns
    lanes = o_ref.shape[3]
    depth = wm_ref.shape[0]
    band = rows * depth
    slots = grid.shape[1]
    share = columns // HALVES
    kept = grid.shape[0]
    reach_one, reach_two = share + 2, share + 2

    loads = [
        pltpu.make_async_copy(source, target, load_sem.at[n])
        for n, (source, target) in enumerate(
            (
                (x_any, x_ref), (wf_any, wf_ref), (wm_any, wm_ref), (wl_any, wl_ref),
                (src_any, src_ref), (tgt_any, tgt_ref), (slot_any, slot_ref),
            )
        )
    ]
    barrier = pltpu.get_barrier_semaphore()
    for step in range(1, groups):
        pl.semaphore_signal(
            barrier, inc=1, device_id={"pair": lax.rem(me + step, groups)}, device_id_type=MESH
        )
    for turn in range(1, rows):
        pl.semaphore_signal(
            barrier, inc=1, device_id={"row": lax.rem(row + turn, rows)}, device_id_type=MESH
        )

    low, high = me, groups - 1 - me
    near, gap = jnp.minimum(low, high), jnp.abs(high - low)

    def distant(step):
        single = jnp.where(high > low, groups - 1 - step, step)
        beyond = step - gap
        away = near - lax.div(beyond, 2)
        double = me + jnp.where(lax.rem(beyond, 2) == 0, away, -away)
        return jnp.where(step < gap, single, double)

    peers = [distant(step) for step in range(groups - 1)]
    routes = [jnp.where(k < me, k, k + 1) for k in range(groups - 1)]

    for load in loads:
        load.start()
    loads[0].wait()

    for image in range(local_images):
        cells = x_ref[image, 0].astype(jnp.float32)
        scale = lax.rsqrt(jnp.sum(cells * cells, axis=-1, keepdims=True) + NORM_EPS)
        normed = (cells * scale).astype(jnp.bfloat16)
        for piece in range(groups):
            parts[piece, image] = normed[:, piece * chunk : (piece + 1) * chunk]
    held[pl.ds(me * local_images, local_images)] = parts[me]
    pl.semaphore_wait(barrier, groups + rows - 2)

    def arrived(where, semaphore):
        pltpu.make_async_remote_copy(
            src_ref=where, dst_ref=where, send_sem=semaphore, recv_sem=semaphore,
            device_id={"row": row}, device_id_type=MESH,
        ).wait_recv()

    def sent(where, semaphore):
        pltpu.make_async_remote_copy(
            src_ref=where, dst_ref=where, send_sem=semaphore, recv_sem=semaphore,
            device_id={"row": row}, device_id_type=MESH,
        ).wait_send()

    def hop(peer, slot):
        return pltpu.make_async_remote_copy(
            src_ref=parts.at[peer],
            dst_ref=held.at[pl.ds(slot * local_images, local_images)],
            send_sem=hop_send.at[0], recv_sem=hop_recv.at[0],
            device_id={"pair": peer}, device_id_type=MESH,
        )

    for to in peers:
        hop(to, me).start()

    grid[...] = jnp.zeros_like(grid)
    block = taps.shape[0] // (kept + 2)
    for edge in (0, kept + 1):
        taps[edge * block : (edge + 1) * block, :] = jnp.zeros((block, lanes), taps.dtype)
    for edge in (0, reach_one + 1):
        first[edge * band : (edge + 1) * band, :] = jnp.zeros((band, lanes), first.dtype)
    for edge in (0, reach_two + 1):
        second[edge * band : (edge + 1) * band, :] = jnp.zeros((band, lanes), second.dtype)

    def select(shape, test):
        i = lax.broadcasted_iota(jnp.int32, shape, 0)
        m = lax.broadcasted_iota(jnp.int32, shape, 1)
        return test(i, m)

    for tap in range(10):
        c, d = tap // 3, tap % 3

        def reaches(i, m):
            line = lax.div(m, columns) + c - 1
            spot = lax.rem(m, columns) + d - 1
            return (i == line * columns + spot) & (line >= 0) & (line < rows) & (spot >= 0) & (spot < columns)

        if tap < 9:
            move = select((lanes, lanes), reaches).astype(jnp.bfloat16)
        else:
            move = jnp.zeros((lanes, lanes), jnp.bfloat16)
        moves[:, tap * lanes : (tap + 1) * lanes] = move

    for load in loads[1:]:
        load.wait()
    count = wf_ref.shape[1]
    kernels = jnp.concatenate([wm_ref[...].reshape(depth * depth, count), wl_ref[...]], axis=0)
    height = kernels.shape[0]
    wide = 2 * lanes
    matching = select((height, wide), lambda i, m: lax.rem(i, depth) == lax.rem(m, depth))
    folding = select((32, height), lambda i, m: lax.div(m, depth) == i).astype(jnp.bfloat16)
    line_of = select((32, wide), lambda i, m: lax.div(lax.rem(m, band), depth))
    last_rows = [[] for _ in range(rows)]
    for tap in range(9):
        here = select(
            (count, wide),
            lambda i, m: (i == (lax.div(lax.rem(m, band), depth) * 3 + lax.div(m, band)) * 9 + tap)
            & (lax.rem(m, band) < 3 * depth)
            & (m < 3 * band),
        ).astype(jnp.bfloat16)
        picks = jnp.dot(kernels, here, preferred_element_type=jnp.float32)
        picks = jnp.where(matching, picks, 0.0).astype(jnp.bfloat16)
        folded = jnp.dot(folding, picks, preferred_element_type=jnp.float32)
        for turn in range(rows):
            shift = ((turn - 1) * depth) % wide
            moved = pltpu.roll(folded, shift, 1) if shift else folded
            moved = jnp.where((line_of >= turn - 1) & (line_of <= turn + 1), moved, 0.0)[:, : 3 * band]
            start = (turn * 9 + tap) * depth
            w2_ref[start : start + depth, :] = moved[:depth].astype(jnp.bfloat16)
            last_rows[turn].append(moved[depth : depth + 1])
    for turn in range(rows):
        last = jnp.concatenate(last_rows[turn] + [jnp.zeros((16 - 9, 3 * band), jnp.float32)], axis=0)
        w3_ref[turn * 16 : (turn + 1) * 16, :] = last.astype(jnp.bfloat16)

    for turn in range(rows):
        def uses(i, m):
            inside = lax.rem(m, block)
            a = lax.rem(inside, rows) - turn + 1
            tap = lax.div(inside, rows)
            return (i == 27 * a + 9 * lax.div(m, block) + tap) & (a >= 0) & (a < 3) & (tap < 9)

        here = select((count, 3 * block), uses).astype(jnp.bfloat16)
        packed = jnp.dot(wf_ref[...], here, preferred_element_type=jnp.float32)
        w1_ref[turn * depth : (turn + 1) * depth, :] = packed.astype(jnp.bfloat16)

    def masks(size):
        place = lax.broadcasted_iota(jnp.int32, (size, lanes), 1)
        line = lax.div(place, columns)
        spot = lax.rem(place, columns)
        lines = [((line + c - 1 >= 0) & (line + c - 1 < rows)).astype(jnp.float32) for c in range(3)]
        spots = [((spot + d - 1 >= 0) & (spot + d - 1 < columns)).astype(jnp.float32) for d in range(3)]
        return lines, spots

    def gathered(term_at, lines, spots):
        summed = None
        for c in range(3):
            inner = None
            for d in range(3):
                term = term_at(c * 3 + d)
                if d != 1:
                    term = pltpu.roll(term, (1 - d) % lanes, 1) * spots[d]
                inner = term if inner is None else inner + term
            if c != 1:
                inner = pltpu.roll(inner, ((1 - c) * columns) % lanes, 1) * lines[c]
            summed = inner if summed is None else summed + inner
        return jnp.maximum(summed, 0.0)

    wanted = {}
    for step, to in enumerate(routes + [me]):
        for pair in range(group_pairs):
            index = to * group_pairs + pair
            wanted[step, pair] = slot_ref[src_ref[index]], slot_ref[tgt_ref[index]]
    arrived(held.at[pl.ds(0, (groups - 1) * local_images)], hop_recv.at[0])

    lot = lax.div(me, HALVES)
    side = lax.rem(me, HALVES)

    def pick(to, pair):
        return pltpu.make_async_remote_copy(
            src_ref=picked.at[to, pair], dst_ref=chosen.at[lot, row],
            send_sem=pick_send.at[0], recv_sem=pick_recv.at[lot],
            device_id={"pair": to, "row": pair * HALVES + side}, device_id_type=MESH,
        )

    def gather_pick(step, to, pair):
        source_slot, target_slot = wanted[step, pair]
        source_image = held[source_slot]
        target_image = held[target_slot]
        picked[to, pair, 0] = source_image
        picked[to, pair, 1] = target_image
        if to is me:
            @pl.when(pair * HALVES + side == row)
            def _():
                pltpu.make_async_copy(picked.at[me, pair], chosen.at[lot, row], pick_recv.at[lot]).start()

    def send_pick(to, pair):
        if to is not me:
            pick(to, pair).start()
        else:
            @pl.when(pair * HALVES + side != row)
            def _():
                pick(to, pair).start()

    turns = [(step, to, pair) for step, to in enumerate(routes + [me]) for pair in reversed(range(group_pairs))]
    for part in (turns[:HEAD], turns[HEAD:]):
        for step, to, pair in part:
            gather_pick(step, to, pair)
        for step, to, pair in part:
            send_pick(to, pair)

    total = jnp.zeros((positions, positions), jnp.float32)
    teams = groups // HALVES
    toward = jnp.where(lot < teams // 2, 1, -1)
    for step in range(teams):
        piece = lax.rem(lot + toward * step + teams, teams)
        arrived(chosen.at[piece], pick_recv.at[piece])
        left = jnp.concatenate([chosen[piece, turn, 0] for turn in range(rows)], axis=0)
        right = jnp.concatenate([chosen[piece, turn, 1] for turn in range(rows)], axis=0)
        total = total + lax.dot_general(
            left, right, (((1,), (1,)), ((), ())), preferred_element_type=jnp.float32
        )
    partial[...] = total.reshape(partial.shape)
    off = columns - kept
    swap = pltpu.make_async_remote_copy(
        src_ref=partial.at[:, pl.ds(pl.multiple_of((1 - half) * off, off), kept)],
        dst_ref=other, send_sem=mate_sem.at[0], recv_sem=mate_sem.at[1],
        device_id={"row": row + 1 - 2 * half}, device_id_type=MESH,
    )
    swap.start()
    swap.wait()
    mine = partial[:, pl.ds(pl.multiple_of(half * off, off), kept), :]
    correlation = (mine + other[...]).astype(jnp.bfloat16).astype(jnp.float32)
    for turn in range(rows):
        grid[:, turn, :] = correlation[turn]
        grid[:, rows + turn, :] = correlation[turn]
    cells = grid[...].reshape(kept * slots, lanes).astype(jnp.bfloat16)
    upper = lax.broadcasted_iota(jnp.int32, (slots, lanes), 0) < rows
    blank = jnp.zeros((slots, lanes), jnp.float32)
    for pack in range(block // 16):
        moved = moves[:, pack * 4 * lanes : min(pack * 4 + 4, 10) * lanes]
        shifted = jnp.dot(cells, moved, preferred_element_type=jnp.float32)
        for j in range(kept):
            piece = shifted[j * slots : (j + 1) * slots]
            pairs = [
                jnp.where(upper, piece[:, n * lanes : (n + 1) * lanes], piece[:, (n + 1) * lanes : (n + 2) * lanes])
                for n in range(0, moved.shape[1] // lanes, 2)
            ]
            both = jnp.concatenate((pairs + [blank])[:2], axis=0)
            start = (j + 1) * block + pack * 16
            taps[start : start + 16, :] = both.astype(jnp.bfloat16)

    def windows(ref, size, first_at):
        return jnp.concatenate(
            [ref[pl.ds(pl.multiple_of((first_at + n) * size, 16), 3 * size), :] for n in range(2)], axis=1
        )

    lead_one = half * (columns - reach_one - off)
    for t in range(0, reach_one, 2):
        product = jnp.dot(w1_ref[...], windows(taps, block, lead_one + t), preferred_element_type=jnp.float32)
        value = jnp.maximum(product, 0.0).astype(jnp.bfloat16)
        for n in range(2):
            first[(t + n + 1) * band : (t + n + 2) * band, :] = value[:, n * lanes : (n + 1) * lanes]

    lines, spots = masks(depth)
    for t in range(0, reach_two, 2):
        window = windows(first, band, (reach_one - reach_two) * half + t)
        for turn in range(rows):
            product = jnp.dot(
                w2_ref[turn * 9 * depth : (turn + 1) * 9 * depth, :], window, preferred_element_type=jnp.float32
            )
            for n in range(2):
                value = gathered(
                    lambda tap: product[tap * depth : (tap + 1) * depth, n * lanes : (n + 1) * lanes], lines, spots
                )
                start = (t + n + 1) * band + turn * depth
                second[start : start + depth, :] = value.astype(jnp.bfloat16)

    for t in range(0, share, 2):
        product = jnp.dot(w3_ref[...], windows(second, band, 2 * half + t), preferred_element_type=jnp.float32)
        for n in range(2):
            third[t + n] = product[:, n * lanes : (n + 1) * lanes]

    lines, spots = masks(share)
    peak = None
    for turn in range(rows):
        value = gathered(lambda tap: third[:, turn * 16 + tap, :], lines, spots)
        scores[turn, :share] = value
        top = jnp.max(value, axis=0, keepdims=True)
        peak = top if peak is None else jnp.maximum(peak, top)
    peak = jnp.broadcast_to(peak, (8, lanes))
    for turn in range(rows):
        scores[turn, share:] = peak

    def give(to):
        return pltpu.make_async_remote_copy(
            src_ref=scores.at[to], dst_ref=got_scores.at[row],
            send_sem=score_send.at[0], recv_sem=score_recv.at[0],
            device_id={"row": to}, device_id_type=MESH,
        )

    others = [(1 - team) * HALVES + n for n in range(HALVES)] + [row + 1 - 2 * half]
    for to in others:
        give(to).start()
    got_scores[row] = scores[row]

    sent(held.at[pl.ds(0, (groups - 1) * local_images)], hop_send.at[0])
    sent(picked.at[pl.ds(0, groups - 1)], pick_send.at[0])
    for pair in range(group_pairs):
        @pl.when(pair * HALVES + side != row)
        def _():
            sent(picked.at[0, 0], pick_send.at[0])

    arrived(got_scores.at[pl.ds(0, rows - 1)], score_recv.at[0])
    for pair in range(group_pairs):
        source_best = got_scores[pair * HALVES, share : share + 1, :]
        for part in range(1, HALVES):
            source_best = jnp.maximum(source_best, got_scores[pair * HALVES + part, share : share + 1, :])
        for part in range(HALVES):
            value = got_scores[pair * HALVES + part, :share]
            target_best = jnp.max(value, axis=-1, keepdims=True)
            o_ref[pair, 0, part * share : (part + 1) * share, :] = (
                value / (source_best + EPSILON) * (value / (target_best + EPSILON))
            ).astype(o_ref.dtype)

    sent(got_scores.at[pl.ds(0, rows - 1)], score_send.at[0])


def spread(features, src_ids, tgt_ids, image_slot, w_first, w_mid, w_last):
    groups = lax.axis_size("pair")
    rows = lax.axis_size("row")
    local_images, _, columns, channels = features.shape
    chunk = channels // groups
    depth = w_mid.shape[1]
    group_pairs = src_ids.shape[0] // groups
    positions = rows * columns
    band = rows * depth
    share = columns // HALVES
    kept = share + 8
    slots = 2 * rows
    block = 48
    vmem = pl.BlockSpec(memory_space=pltpu.VMEM)
    dma = pltpu.SemaphoreType.DMA
    bf16, f32 = jnp.bfloat16, jnp.float32
    weights = (w_first.transpose(2, 1, 0)[0], w_mid.transpose(1, 2, 0), w_last.transpose(1, 2, 0)[0])
    result = pl.pallas_call(
        spread_kernel,
        out_shape=pltpu.VMEM((group_pairs, 1, columns, positions), f32),
        in_specs=[pl.BlockSpec(memory_space=pltpu.HBM)] * 7,
        out_specs=vmem,
        scratch_shapes=[
            pltpu.VMEM(features.shape, bf16),
            *(pltpu.VMEM(weight.shape, bf16) for weight in weights),
            *(pltpu.SMEM(ids.shape, jnp.int32) for ids in (src_ids, tgt_ids, image_slot)),
            dma((7,)),
            pltpu.VMEM((band, 3 * block), bf16),
            pltpu.VMEM((9 * band, 3 * band), bf16),
            pltpu.VMEM((rows * 16, 3 * band), bf16),
            pltpu.VMEM((positions, 10 * positions), bf16),
            pltpu.VMEM((groups, local_images, columns, chunk), bf16),
            pltpu.VMEM((groups * local_images, columns, chunk), bf16),
            pltpu.VMEM((groups, group_pairs, 2, columns, chunk), bf16),
            pltpu.VMEM((groups // HALVES, rows, 2, columns, chunk), bf16),
            pltpu.VMEM((rows, columns, positions), f32),
            pltpu.VMEM((rows, kept, positions), f32),
            pltpu.VMEM((kept, slots, positions), f32),
            pltpu.VMEM(((kept + 2) * block, positions), bf16),
            pltpu.VMEM(((share + 4) * band, positions), bf16),
            pltpu.VMEM(((share + 4) * band, positions), bf16),
            pltpu.VMEM((share, rows * 16, positions), f32),
            pltpu.VMEM((rows, share + 8, positions), f32),
            pltpu.VMEM((rows, share + 8, positions), f32),
            dma((1,)), dma((1,)),
            dma((1,)), dma((groups // HALVES,)),
            dma((2,)),
            dma((1,)), dma((1,)),
        ],
        compiler_params=pltpu.CompilerParams(
            collective_id=0, has_side_effects=True, vmem_limit_bytes=VMEM_LIMIT
        ),
    )(*(pltpu.with_memory_space_constraint(x, pltpu.HBM) for x in (features, *weights, src_ids, tgt_ids, image_slot)))
    return result.astype(bf16)


def program(features, src_ids, tgt_ids, image_slot, w_first, w_mid, w_last):
    groups = lax.axis_size("pair")
    rows = lax.axis_size("row")
    _, local_rows, columns, channels = features.shape
    fits = (
        local_rows == 1
        and groups % HALVES == 0
        and rows * groups == HALVES * src_ids.shape[0]
        and channels % (groups * 128) == 0
        and rows * columns == 128
        and columns == 32
        and rows == 2 * HALVES
        and w_mid.shape[1] == 16
    )
    run = spread if fits else local
    return run(features, src_ids, tgt_ids, image_slot, w_first, w_mid, w_last)


def solution(mesh):
    placed = (P("pair", "row", None, None), P(), P(), P(), P(), P(), P())
    return jax.shard_map(
        program, mesh=mesh, in_specs=placed, out_specs=P("pair", "row", None, None), check_vma=False
    )
```
